32 devices in a mesh: circ: 8 (over y, x, core), axial: 4 (over z).
Axes of the slice: x: 2, y: 2, z: 4, core: 2. Of those that a mesh axis runs over, the one named last changes fastest.
Arguments:
- electric: float32 [3, 8, 128, 1024], P(None, None, 'circ', 'axial'), may hold values from -6 to 6
- magnetic: float32 [3, 8, 128, 1024], P(None, None, 'circ', 'axial'), may hold values from -6 to 6
- adjoint_electric: float32 [3, 8, 128, 1024], P(None, None, 'circ', 'axial'), may hold values from -6 to 6
- adjoint_magnetic: float32 [3, 8, 128, 1024], P(None, None, 'circ', 'axial'), may hold values from -6 to 6
- electric_diagonal: float32 [3, 8, 128, 1024], P(None, None, 'circ', 'axial'), may hold values from 1 to 2
- electric_coupling: float32 [3, 8, 128, 1024], P(None, None, 'circ', 'axial'), may hold values from -0.4 to 0.4
- magnetic_diagonal: float32 [3, 8, 128, 1024], P(None, None, 'circ', 'axial'), may hold values from 1 to 2
- magnetic_coupling: float32 [3, 8, 128, 1024], P(None, None, 'circ', 'axial'), may hold values from -0.4 to 0.4
- seam_source: int32 [32, 32], P(('circ', 'axial')), may hold values from 0 to 31
- seam_target: int32 [32, 32], P(('circ', 'axial')), may hold values from 0 to 31
- seam_device: int32 [32, 32, 1], P(('circ', 'axial')), may hold values from 0 to 31; in each aligned block of 32 rows (0 to 31, 32 to 63, ..., all dimensions but the last counted through in order) at most 2 rows name the same one
- seam_flip: int32 [32, 32], P(('circ', 'axial')), may hold values from 0 to 1
- seam_count: int32 [32], P(('circ', 'axial')), may hold values from 24 to 32, as said below
Outputs:
- final_electric: float32 [3, 8, 128, 1024], P(None, None, 'circ', 'axial')
- final_magnetic: float32 [3, 8, 128, 1024], P(None, None, 'circ', 'axial')
- backward_electric: float32 [3, 8, 128, 1024], P(None, None, 'circ', 'axial')
- backward_magnetic: float32 [3, 8, 128, 1024], P(None, None, 'circ', 'axial')
- sensitivity: float32 [3, 8, 128, 1024], P(None, None, 'circ', 'axial')
The draws below stay inside these ranges and needn't reach their ends.
Inputs may be any that keep to these rules, and one draw needn't show every extreme that they name: `seam_device`: among the slots of one device no receiving device appears more than 2 times, and some receiving device appears exactly 2 times. Slots of a device from seam_count on are unused; some device uses all 32.
All inputs are finite; a program needn't handle non-finite values.
Results may differ from the reference program's by a relative error of at most 0.0001.
Values sent between devices are 32-bit elements; how exact they have to be, the bound alone decides.
A program may use at most 128 MiB of HBM per device.

```python
import math
import jax
import jax.numpy as jnp
import numpy as np

LAYERS = 8
CC = 16
CA = 256
STEPS = 4
CAP = 2
SEAMS = 32
FACE_BLOCKS = 32
NC = 128
NA = 1024
N_CIRC = 8
N_AXIAL = 4


def draw_seam_count(key, part):
    first_key, second_key = jax.random.split(jax.random.fold_in(key, 11))
    counts = jax.random.randint(first_key, (SEAMS,), 3 * SEAMS // 4, SEAMS + 1)
    chosen = jax.random.randint(second_key, (), 0, SEAMS)
    return jnp.where(jnp.arange(SEAMS) == chosen, SEAMS, counts).astype(jnp.int32)


def touch_ends(result, rng, low, high):
    shape = result.shape
    index_at = [jax.random.randint(jax.random.fold_in(rng, axis), (), 0, shape[axis]) for axis in range(len(shape))]
    result = result.at[tuple(index_at)].set(low)
    longest = shape.index(max(shape))
    index_at[longest] = (index_at[longest] + 1) % shape[longest]
    return result.at[tuple(index_at)].set(high)


def shard_levels(stream_key, extent, cuts, least, high):
    gain, own = 1.0, jax.random.fold_in(stream_key, 6)
    for position, parts in cuts:
        heights = jnp.exp(jax.random.uniform(jax.random.fold_in(own, position), (parts,), jnp.float32, least / len(cuts), high / len(cuts)))
        gain = gain * jnp.repeat(heights, extent[position] // parts).reshape([-1 if axis == position else 1 for axis in range(len(extent))])
    return gain


def shared_out(rng, own, number, rows, number_of, top, most, skew):
    sequence = jax.random.permutation(rng, number_of)
    heavy_load, usual = load_shares(number_of, rows * top, most, skew, True), load_shares(number_of, rows * top, most, skew, False)
    places = jnp.arange(number_of)

    def named(tallies, offset_by):
        used = int((tallies > 0).sum())
        fixed = max(1, used // 4)
        moved = fixed + (places - fixed + offset_by * (used - fixed)) % max(1, number_of - fixed)
        return jnp.zeros((number_of,), jnp.int32).at[sequence[jnp.where(places < fixed, places, moved)]].set(jnp.asarray(tallies, jnp.int32))

    tallies = jnp.where(number % 4 == 0, named(heavy_load, number // 4), named(usual, number - number // 4 - 1))
    mixed = jax.random.permutation(jax.random.fold_in(own, 3), number_of)
    giver, taker = mixed[0:number_of // 2 * 2:2], mixed[1:number_of // 2 * 2:2]
    slack = jnp.minimum(tallies[giver] - 1, most - tallies[taker]) // 2
    slack = jnp.where((giver == sequence[0]) | (taker == sequence[0]) | (tallies[taker] == 0), 0, jnp.maximum(slack, 0))
    moved = jax.random.randint(jax.random.fold_in(own, 4), (number_of // 2,), 0, 1 << 20) % (slack + 1)
    tallies = tallies.at[giver].add(-moved).at[taker].add(moved)
    items = jnp.searchsorted(jnp.cumsum(tallies), jnp.arange(rows * top), side="right").astype(jnp.int32)
    grid = items.reshape(top, rows).T
    grid = grid[jax.random.permutation(jax.random.fold_in(own, 1), rows)]
    offset_by = jax.random.randint(jax.random.fold_in(own, 2), (rows, 1), 0, top)
    return jnp.take_along_axis(grid, (jnp.arange(top)[None, :] + offset_by) % top, axis=1)


def load_shares(amount, total, limit, slope, full):
    loads = [(1 << 20) // math.isqrt(standing ** slope) + 1 for standing in range(1, amount + 1)]
    largest = limit if full else min(limit, max(-(-total // amount), total * loads[0] // sum(loads)))
    least = 1 if total - largest >= amount - 1 else 0
    given, surplus = [largest] + [least] * (amount - 1), total - largest - least * (amount - 1)
    while surplus > 0:
        candidates = [i for i in range(1, amount) if given[i] < largest] or [i for i in range(1, amount) if given[i] < limit]
        pool, left = sum([loads[i] for i in candidates]), surplus
        for i in candidates:
            extra = min(limit - given[i], max(1, left * loads[i] // pool), surplus)
            given[i] = given[i] + extra
            surplus = surplus - extra
    return np.array(given)


def normal_values(own_key, shape, deviation, limit, shards=(), held_as=jnp.bfloat16):
    array = deviation * jax.random.normal(own_key, shape, jnp.float32)
    if shards:
        array = array * shard_levels(own_key, shape, shards, -0.22, 0.18)
    return jnp.clip(array, -limit, limit).astype(held_as)


def setup_inputs(seed: int = 0) -> dict:
    key_list = jax.random.split(jax.random.key(seed), 14)
    electric = normal_values(key_list[0], (3, LAYERS, NC, NA), 1.0, 6.0, ((2, 8), (3, 4)), jnp.float32)
    magnetic = normal_values(key_list[1], (3, LAYERS, NC, NA), 1.0, 6.0, ((2, 8), (3, 4)), jnp.float32)
    adjoint_electric = normal_values(key_list[2], (3, LAYERS, NC, NA), 1.0, 6.0, ((2, 8), (3, 4)), jnp.float32)
    adjoint_magnetic = normal_values(key_list[3], (3, LAYERS, NC, NA), 1.0, 6.0, ((2, 8), (3, 4)), jnp.float32)
    electric_diagonal = jnp.clip(1.0 + 1.0 * jax.random.uniform(key_list[4], (3, LAYERS, NC, NA), jnp.float32) ** shard_levels(key_list[4], (3, LAYERS, NC, NA), ((2, 8), (3, 4)), -0.2, 0.2), 1.0, 2.0)
    electric_coupling = jnp.clip(jax.random.uniform(key_list[5], (3, LAYERS, NC, NA), jnp.float32, -0.4, 0.4) * shard_levels(key_list[5], (3, LAYERS, NC, NA), ((2, 8), (3, 4)), -0.4, 0.0), -0.4, 0.4)
    magnetic_diagonal = jnp.clip(1.0 + 1.0 * jax.random.uniform(key_list[6], (3, LAYERS, NC, NA), jnp.float32) ** shard_levels(key_list[6], (3, LAYERS, NC, NA), ((2, 8), (3, 4)), -0.2, 0.2), 1.0, 2.0)
    magnetic_coupling = jnp.clip(jax.random.uniform(key_list[7], (3, LAYERS, NC, NA), jnp.float32, -0.4, 0.4) * shard_levels(key_list[7], (3, LAYERS, NC, NA), ((2, 8), (3, 4)), -0.4, 0.0), -0.4, 0.4)
    seam_source = touch_ends(jax.random.randint(key_list[8], (SEAMS, SEAMS), 0, FACE_BLOCKS), jax.random.fold_in(key_list[8], 1), 0, FACE_BLOCKS - 1).astype(jnp.int32)
    seam_target = touch_ends(jax.random.randint(key_list[9], (SEAMS, SEAMS), 0, FACE_BLOCKS), jax.random.fold_in(key_list[9], 1), 0, FACE_BLOCKS - 1).astype(jnp.int32)
    seam_device_keys = jax.random.split(jax.random.fold_in(key_list[10], 1), SEAMS * SEAMS // SEAMS)
    seam_device_turns = jax.random.permutation(jax.random.fold_in(key_list[10], 3), SEAMS * SEAMS // SEAMS)
    seam_device = jax.vmap(lambda own, number: shared_out(jax.random.fold_in(key_list[10], 2), own, number, SEAMS, SEAMS, 1, CAP, 2))(seam_device_keys, seam_device_turns).reshape((SEAMS, SEAMS, 1))
    seam_flip = touch_ends(jax.random.randint(key_list[11], (SEAMS, SEAMS), 0, 2), jax.random.fold_in(key_list[11], 1), 0, 1).astype(jnp.int32)
    seam_count = draw_seam_count(jax.random.fold_in(key_list[13], 71), 0)
    return dict(electric=electric, magnetic=magnetic, adjoint_electric=adjoint_electric, adjoint_magnetic=adjoint_magnetic, electric_diagonal=electric_diagonal, electric_coupling=electric_coupling, magnetic_diagonal=magnetic_diagonal, magnetic_coupling=magnetic_coupling, seam_source=seam_source, seam_target=seam_target, seam_device=seam_device, seam_flip=seam_flip, seam_count=seam_count)


time_step = 0.18


def apply_metric(diagonal, coupling, fields):
    radial = diagonal[0] * fields[0] + coupling[0] * fields[1] + coupling[1] * fields[2]
    beside_all = coupling[0] * fields[0] + diagonal[1] * fields[1] + coupling[2] * fields[2]
    lengthwise = coupling[1] * fields[0] + coupling[2] * fields[1] + diagonal[2] * fields[2]
    return jnp.stack([radial, beside_all, lengthwise])


def seam_ghosts(fields, seam_source, seam_target, seam_device, seam_flip, seam_count):
    devices = N_CIRC * N_AXIAL
    halves = CA // 128
    surface = fields[1:3, -1].reshape(2, N_CIRC, CC, N_AXIAL, halves, 128)
    surface = surface.transpose(1, 3, 2, 4, 0, 5).reshape(devices, FACE_BLOCKS, 2, 128)
    picked = jnp.take_along_axis(surface, seam_source[:, :, None, None], axis=1)
    turned = jnp.stack([picked[:, :, 0, ::-1], -picked[:, :, 1, ::-1]], axis=2)
    oriented = jnp.where(seam_flip[:, :, None, None] == 1, turned, picked)
    active = (jnp.arange(SEAMS)[None, :] < seam_count[:, None]).astype(jnp.float32)
    oriented = oriented * active[:, :, None, None]
    target = seam_device[:, :, 0] * FACE_BLOCKS + seam_target
    summed = jax.ops.segment_sum(oriented.reshape(-1, 2, 128), target.reshape(-1), num_segments=devices * FACE_BLOCKS)
    summed = summed.reshape(N_CIRC, N_AXIAL, CC, halves, 2, 128).transpose(4, 0, 2, 1, 3, 5)
    return summed.reshape(2, N_CIRC * CC, N_AXIAL * CA)


def forward_around(values):
    return jnp.roll(values, -1, axis=1) - values


def forward_lengthwise(values):
    return jnp.concatenate([values[:, :, 1:], jnp.zeros_like(values[:, :, :1])], axis=2) - values


def forward_radial(values, border):
    return jnp.concatenate([values[1:], border[None]], axis=0) - values


def backward_around(values):
    return values - jnp.roll(values, 1, axis=1)


def backward_lengthwise(values):
    return values - jnp.concatenate([jnp.zeros_like(values[:, :, :1]), values[:, :, :-1]], axis=2)


def backward_radial(values):
    return values - jnp.concatenate([jnp.zeros_like(values[:1]), values[:-1]], axis=0)


def curl_forward(fields, ghosts):
    radial = forward_around(fields[2]) - forward_lengthwise(fields[1])
    beside_all = forward_lengthwise(fields[0]) - forward_radial(fields[2], ghosts[1])
    lengthwise = forward_radial(fields[1], ghosts[0]) - forward_around(fields[0])
    return jnp.stack([radial, beside_all, lengthwise])


def curl_backward(fields):
    radial = backward_around(fields[2]) - backward_lengthwise(fields[1])
    beside_all = backward_lengthwise(fields[0]) - backward_radial(fields[2])
    lengthwise = backward_radial(fields[1]) - backward_around(fields[0])
    return jnp.stack([radial, beside_all, lengthwise])


def reference(electric, magnetic, adjoint_electric, adjoint_magnetic, electric_diagonal, electric_coupling, magnetic_diagonal, magnetic_coupling, seam_source, seam_target, seam_device, seam_flip, seam_count):
    def ghosts_of(fields):
        return seam_ghosts(fields, seam_source, seam_target, seam_device, seam_flip, seam_count)

    history = []
    for moment in range(STEPS):
        history.append(electric)
        magnetic = magnetic - time_step * apply_metric(magnetic_diagonal, magnetic_coupling, curl_forward(electric, ghosts_of(electric)))
        electric = electric + time_step * apply_metric(electric_diagonal, electric_coupling, curl_backward(magnetic))
    sensitivity = jnp.zeros_like(electric)
    back_electric = adjoint_electric
    back_magnetic = adjoint_magnetic
    for moment in reversed(range(STEPS)):
        back_electric = back_electric - time_step * apply_metric(electric_diagonal, electric_coupling, curl_backward(back_magnetic))
        back_magnetic = back_magnetic + time_step * apply_metric(magnetic_diagonal, magnetic_coupling, curl_forward(back_electric, ghosts_of(back_electric)))
        sensitivity = sensitivity + history[moment] * back_electric
    return (electric, magnetic, back_electric, back_magnetic, sensitivity)
```

```python
import functools

import jax
import jax.numpy as jnp
from jax import lax
from jax.experimental import pallas as pl
from jax.experimental.pallas import tpu as pltpu
from jax.sharding import PartitionSpec as P

STEPS = 4
CAP = 2
TIME_STEP = 0.18
MESH = pl.DeviceIdType.MESH
LANES = 128

EF, HB, AF, GB = range(4)


def pieces(x):
    high = x.astype(jnp.bfloat16)
    rest = x - high.astype(jnp.float32)
    mid = rest.astype(jnp.bfloat16)
    low = (rest - mid.astype(jnp.float32)).astype(jnp.bfloat16)
    return jnp.concatenate([high, mid, low], axis=0)


def picked_dot(matrix, x):
    return jnp.dot(matrix, pieces(x), preferred_element_type=jnp.float32)


def kernel(
    shape,
    n_circ,
    n_axial,
    e_in,
    h_in,
    a_in,
    g_in,
    ed_in,
    ec_in,
    md_in,
    mc_in,
    source_in,
    target_in,
    device_in,
    flip_in,
    count_in,
    e,
    h,
    a,
    g,
    sens,
    e_hist,
    a_hist,
    ed,
    ec,
    md,
    mc,
    row_send,
    row_recv,
    col_send,
    col_recv,
    seam_send,
    seam_recv,
    land_send,
    land_recv,
    gather_mat,
    scatter_mat,
    source_ref,
    target_ref,
    device_ref,
    flip_ref,
    count_ref,
    in_sems,
    map_sems,
    row_ssem,
    row_rsem,
    col_ssem,
    col_rsem,
    seam_ssem,
    seam_rsem,
    land_sems,
):
    layers, cc, ca = shape
    halves = ca // LANES
    subs = cc // 8
    n_dev = n_circ * n_axial
    rows = n_dev * CAP * 2
    cols = 2 * halves * cc
    ci = lax.axis_index("circ")
    ai = lax.axis_index("axial")
    me = ci * n_axial + ai

    barrier = pltpu.get_barrier_semaphore()
    partners = [
        (dc, da)
        for da in reversed(range(n_axial))
        for dc in reversed(range(n_circ))
        if dc or da
    ]

    def peer_of(dc, da):
        return lax.bitwise_xor(ci, dc), lax.bitwise_xor(ai, da)

    col_recv[...] = jnp.zeros_like(col_recv)
    for dc, da in partners:
        pl.semaphore_signal(barrier, inc=1, device_id=peer_of(dc, da), device_id_type=MESH)

    loads = [
        pltpu.make_async_copy(src, dst, in_sems.at[i])
        for i, (src, dst) in enumerate(
            [
                (e_in, e),
                (g_in, g),
                (a_in, a),
                (ed_in, ed),
                (ec_in, ec),
                (md_in, md),
                (mc_in, mc),
                (h_in, h),
                (e_in, e_hist.at[0]),
            ]
        )
    ]
    maps = [
        pltpu.make_async_copy(src, dst, map_sems.at[i])
        for i, (src, dst) in enumerate(
            [
                (source_in, source_ref),
                (target_in, target_ref),
                (device_in, device_ref),
                (flip_in, flip_ref),
                (count_in, count_ref),
            ]
        )
    ]
    for load in maps + loads:
        load.start()

    def all_to_all(send, recv, ssem, rsem):
        for dc, da in partners:
            pc, pa = peer_of(dc, da)
            pltpu.make_async_remote_copy(
                src_ref=send.at[pc * n_axial + pa],
                dst_ref=recv.at[me],
                send_sem=ssem,
                recv_sem=rsem,
                device_id=(pc, pa),
                device_id_type=MESH,
            ).start()
        recv[pl.ds(me, 1)] = send[pl.ds(me, 1)]

    def all_to_all_done(send, recv, ssem, rsem):
        return pltpu.make_async_remote_copy(
            src_ref=send.at[pl.ds(0, n_dev - 1)],
            dst_ref=recv.at[pl.ds(0, n_dev - 1)],
            send_sem=ssem,
            recv_sem=rsem,
            device_id=(ci, ai),
            device_id_type=MESH,
        )

    lane8 = lax.broadcasted_iota(jnp.int32, (8, LANES), 1)

    def row_copy(kind, t, step):
        peer = lax.rem(ci + step + n_circ, n_circ)
        return pltpu.make_async_remote_copy(
            src_ref=row_send.at[kind, t],
            dst_ref=row_recv.at[kind, t],
            send_sem=row_ssem.at[kind, t],
            recv_sem=row_rsem.at[kind, t],
            device_id=(peer, ai),
            device_id_type=MESH,
        )

    def col_copy(kind, t, step):
        peer = lax.rem(ai + step + n_axial, n_axial)
        return pltpu.make_async_remote_copy(
            src_ref=col_send.at[kind, t],
            dst_ref=col_recv.at[kind, t],
            send_sem=col_ssem.at[kind, t],
            recv_sem=col_rsem.at[kind, t],
            device_id=(ci, peer),
            device_id_type=MESH,
        )

    def pack_halos(field, kind, t, step, levels):
        edge_row = 0 if step < 0 else cc - 1
        for part, c in enumerate((0, 2)):
            for l in levels:
                at = part * layers + l
                row_send[kind, t, at : at + 1, :] = field[c, l, edge_row : edge_row + 1, :]
        packed = jnp.zeros((8, LANES), jnp.float32) if levels[0] == 0 else col_send[kind, t]
        for c in range(2):
            for l in levels:
                for s in range(subs):
                    k = (c * layers + l) * subs + s
                    lo = 0 if step < 0 else ca - LANES
                    tile = field[c, l, s * 8 : s * 8 + 8, lo : lo + LANES]
                    shift = k if step < 0 else (k + 1) % LANES
                    if shift:
                        tile = pltpu.roll(tile, shift, 1)
                    packed = jnp.where(lane8 == k, tile, packed)
        col_send[kind, t] = packed

    def start_halos(kind, t, step):
        row_copy(kind, t, step).start()

        @pl.when((ai > 0) if step < 0 else (ai < n_axial - 1))
        def _():
            col_copy(kind, t, step).start()

    def wait_halos(kind, t, step):
        row_copy(kind, t, step).wait_recv()

        @pl.when((ai < n_axial - 1) if step < 0 else (ai > 0))
        def _():
            col_copy(kind, t, step).wait_recv()

    def drain_halos(kind, t, step):
        row_copy(kind, t, step).wait_send()

        @pl.when((ai > 0) if step < 0 else (ai < n_axial - 1))
        def _():
            col_copy(kind, t, step).wait_send()

    def pack_seams(field, chain, t):
        surface = jnp.concatenate(
            [
                field[c, layers - 1, :, h * LANES : (h + 1) * LANES]
                for c in (1, 2)
                for h in range(halves)
            ],
            axis=0,
        )
        ends = LANES - 1 - lax.broadcasted_iota(jnp.int32, surface.shape, 1)
        mirrored = jnp.take_along_axis(surface, ends, axis=1)
        out = picked_dot(gather_mat[...], jnp.concatenate([surface, mirrored], axis=0))
        seam_send[chain, t] = out.reshape(n_dev, 2 * CAP, LANES)

    def start_seams(chain, t):
        all_to_all(
            seam_send.at[chain, t],
            seam_recv.at[chain, t],
            seam_ssem.at[chain, t],
            seam_rsem.at[chain, t],
        )

    def ghosts_of(chain, t):
        send, recv = seam_send.at[chain, t], seam_recv.at[chain, t]
        all_to_all_done(send, recv, seam_ssem.at[chain, t], seam_rsem.at[chain, t]).wait_recv()
        ghosts = picked_dot(scatter_mat[...], recv[...].reshape(rows, LANES))
        return [
            jnp.concatenate(
                [
                    ghosts[(c * halves + h) * cc : (c * halves + h + 1) * cc]
                    for h in range(halves)
                ],
                axis=1,
            )
            for c in range(2)
        ]

    sub = lax.broadcasted_iota(jnp.int32, (cc, ca), 0)
    lane = lax.broadcasted_iota(jnp.int32, (cc, ca), 1)

    def column_halo(packed, c, l, last):
        parts = []
        for s in range(subs):
            k = (c * layers + l) * subs + s
            shift = (LANES - 1 - k if last else -k) % LANES
            parts.append(pltpu.roll(packed, shift, 1) if shift else packed)
        halo = jnp.concatenate(parts, axis=0)
        return jnp.concatenate([halo] * halves, axis=1)

    def metric(diagonal, coupling, l, x, y, z):
        d0, d1, d2 = (diagonal[i, l] for i in range(3))
        o0, o1, o2 = (coupling[i, l] for i in range(3))
        return (
            d0 * x + o0 * y + o1 * z,
            o0 * x + d1 * y + o2 * z,
            o1 * x + o2 * y + d2 * z,
        )

    def forward_update(field, new, kind, chain, t, scale, levels):
        packed = col_recv[kind, t]
        for l in levels:
            v0, v1, v2 = (field[i, l] for i in range(3))
            if l + 1 < layers:
                n1, n2 = field[1, l + 1], field[2, l + 1]
            else:
                n1, n2 = ghosts_of(chain, t)

            def around(v, part):
                row = row_recv[kind, t, part * layers + l : part * layers + l + 1, :]
                return jnp.where(sub == cc - 1, row, pltpu.roll(v, cc - 1, 0)) - v

            def along(v, c):
                halo = column_halo(packed, c, l, True)
                return jnp.where(lane == ca - 1, halo, pltpu.roll(v, ca - 1, 1)) - v

            x = around(v2, 1) - along(v1, 1)
            y = along(v0, 0) - (n2 - v2)
            z = (n1 - v1) - around(v0, 0)
            change = metric(md, mc, l, x, y, z)
            for i in range(3):
                new[i, l] = new[i, l] + scale * change[i]

    def backward_update(field, new, kept, kind, t, scale, levels):
        packed = col_recv[kind, t]
        for l in levels:
            v0, v1, v2 = (field[i, l] for i in range(3))

            def around(v, part):
                row = row_recv[kind, t, part * layers + l : part * layers + l + 1, :]
                return v - jnp.where(sub == 0, row, pltpu.roll(v, 1, 0))

            def along(v, c):
                halo = column_halo(packed, c, l, False)
                return v - jnp.where(lane == 0, halo, pltpu.roll(v, 1, 1))

            r1 = v1 - field[1, l - 1] if l else v1
            r2 = v2 - field[2, l - 1] if l else v2
            x = around(v2, 1) - along(v1, 1)
            y = along(v0, 0) - r2
            z = r1 - around(v0, 0)
            change = metric(ed, ec, l, x, y, z)
            for i in range(3):
                value = new[i, l] + scale * change[i]
                new[i, l] = value
                if kept is not None:
                    kept[i, l] = value

    seams = source_ref.shape[1]
    for load in maps:
        load.wait()
    device = device_ref[...]
    count = count_ref[0]
    slot_row = lax.broadcasted_iota(jnp.int32, (1, seams), 1)
    si = lax.broadcasted_iota(jnp.int32, (seams, seams), 0)
    sj = lax.broadcasted_iota(jnp.int32, (seams, seams), 1)
    device_f = device.astype(jnp.float32)
    device_col = jnp.sum(
        jnp.where(si == sj, jnp.broadcast_to(device_f, (seams, seams)), 0.0), axis=1, keepdims=True
    )
    earlier = (device_col == device_f) & (si < sj)
    rank = jnp.sum(jnp.where(earlier, 1.0, 0.0), axis=0, keepdims=True)
    code = jnp.where(slot_row < count, device_f * CAP + rank, -1.0)
    ri = lax.broadcasted_iota(jnp.int32, (rows, seams), 0)
    place = lax.div(ri, 2).astype(jnp.float32) == code

    def picked(values):
        return jnp.sum(
            jnp.where(place, values.astype(jnp.float32), 0.0), axis=1, keepdims=True
        ).astype(jnp.int32)

    comp = lax.rem(lax.broadcasted_iota(jnp.int32, (rows, 1), 0), 2)

    def column_of(block):
        return (comp * halves + lax.rem(block, halves)) * cc + lax.div(block, halves)

    valid = jnp.sum(jnp.where(place, 1.0, 0.0), axis=1, keepdims=True) > 0.5
    landing = jnp.where(valid, column_of(picked(target_ref[...])), -1).astype(jnp.float32)
    land_send[...] = jnp.broadcast_to(landing, (rows, LANES)).reshape(n_dev, 2 * CAP, LANES)
    flipped = picked(flip_ref[...]) == 1
    src_col = jnp.where(valid, column_of(picked(source_ref[...])) + jnp.where(flipped, cols, 0), -1)
    sign = jnp.where(flipped & (comp == 1), -1.0, 1.0)
    ki = lax.broadcasted_iota(jnp.int32, (rows, 2 * cols), 1)
    gather = jnp.where(ki == src_col, sign, 0.0).astype(jnp.bfloat16)
    gather_mat[...] = jnp.concatenate([gather] * 3, axis=1)

    inner, last = list(range(layers - 1)), [layers - 1]
    loads[0].wait()
    pack_seams(e, 0, 0)
    pack_halos(e, EF, 0, -1, inner + last)
    loads[1].wait()
    pack_halos(g, GB, 0, 1, inner + last)
    pl.semaphore_wait(barrier, n_dev - 1)
    start_halos(GB, 0, 1)
    start_seams(0, 0)
    start_halos(EF, 0, -1)
    all_to_all(land_send, land_recv, land_sems.at[0], land_sems.at[1])
    for load in loads[2:]:
        load.wait()

    def step(t, carry):
        wait_halos(GB, t, 1)
        backward_update(g, a, a_hist.at[STEPS - 1 - t], GB, t, -TIME_STEP, last)
        pack_seams(a, 1, t)
        start_seams(1, t)
        backward_update(g, a, a_hist.at[STEPS - 1 - t], GB, t, -TIME_STEP, inner)
        pack_halos(a, AF, t, -1, inner + last)
        start_halos(AF, t, -1)

        @pl.when(t == 0)
        def _():
            all_to_all_done(land_send, land_recv, land_sems.at[0], land_sems.at[1]).wait_recv()
            li = lax.broadcasted_iota(jnp.int32, (rows, LANES), 1).astype(jnp.float32)
            spread = jnp.where(land_recv[...].reshape(rows, LANES) == li, 1.0, 0.0)
            scatter = spread.T[:cols].astype(jnp.bfloat16)
            scatter_mat[...] = jnp.concatenate([scatter] * 3, axis=1)

        wait_halos(EF, t, -1)
        forward_update(e, h, EF, 0, t, -TIME_STEP, inner)
        pack_halos(h, HB, t, 1, inner)
        forward_update(e, h, EF, 0, t, -TIME_STEP, last)
        pack_halos(h, HB, t, 1, last)
        start_halos(HB, t, 1)

        @pl.when(t == STEPS - 1)
        def _():
            for l in range(layers):
                for i in range(3):
                    total = e_hist[STEPS - 1, i, l] * a_hist[STEPS - 1, i, l]
                    for n in reversed(range(STEPS - 1)):
                        total = total + e_hist[n, i, l] * a_hist[n, i, l]
                    sens[i, l] = total

        wait_halos(AF, t, -1)
        forward_update(a, g, AF, 1, t, TIME_STEP, inner)

        @pl.when(t + 1 < STEPS)
        def _():
            pack_halos(g, GB, t + 1, 1, inner)

        forward_update(a, g, AF, 1, t, TIME_STEP, last)

        @pl.when(t + 1 < STEPS)
        def _():
            pack_halos(g, GB, t + 1, 1, last)
            start_halos(GB, t + 1, 1)
            wait_halos(HB, t, 1)
            backward_update(h, e, e_hist.at[t + 1], HB, t, TIME_STEP, last)
            pack_seams(e, 0, t + 1)
            start_seams(0, t + 1)
            backward_update(h, e, e_hist.at[t + 1], HB, t, TIME_STEP, inner)
            pack_halos(e, EF, t + 1, -1, inner + last)
            start_halos(EF, t + 1, -1)

        return carry

    lax.fori_loop(0, STEPS, step, 0)

    wait_halos(HB, STEPS - 1, 1)
    backward_update(h, e, None, HB, STEPS - 1, TIME_STEP, inner + last)

    def drain(t, carry):
        for kind, way in ((EF, -1), (HB, 1), (AF, -1), (GB, 1)):
            drain_halos(kind, t, way)
        for chain in range(2):
            all_to_all_done(
                seam_send.at[chain, t],
                seam_recv.at[chain, t],
                seam_ssem.at[chain, t],
                seam_rsem.at[chain, t],
            ).wait_send()
        return carry

    lax.fori_loop(0, STEPS, drain, 0)
    all_to_all_done(land_send, land_recv, land_sems.at[0], land_sems.at[1]).wait_send()


def copy_out(*refs):
    sources, targets, sems = refs[:5], refs[5:10], refs[10]
    stores = [
        pltpu.make_async_copy(src, dst, sems.at[i])
        for i, (src, dst) in enumerate(zip(sources, targets))
    ]
    for store in stores:
        store.start()
    for store in stores:
        store.wait()


def shards(n_circ, n_axial, *args):
    fields, (source, target, device, flip, count) = args[:8], args[8:]
    block = fields[0].shape
    layers, cc, ca = block[1:]
    n_dev = n_circ * n_axial
    rows = n_dev * CAP * 2
    cols = 2 * (ca // LANES) * cc
    operands = [*fields, source, target, device.reshape(1, -1), flip]
    f32 = jnp.float32
    dma = pltpu.SemaphoreType.DMA
    hbm_spec = pl.BlockSpec(memory_space=pltpu.HBM)
    vmem_spec = pl.BlockSpec(memory_space=pltpu.VMEM)
    results = pl.pallas_call(
        functools.partial(kernel, (layers, cc, ca), n_circ, n_axial),
        out_shape=[pltpu.VMEM(block, f32)] * 5,
        in_specs=[hbm_spec] * 12 + [pl.BlockSpec(memory_space=pl.ANY)],
        out_specs=[vmem_spec] * 5,
        scratch_shapes= [pltpu.VMEM((STEPS,) + block, f32)] * 2
        + [pltpu.VMEM(block, f32)] * 4
        + [pltpu.VMEM((4, STEPS, 2 * layers, ca), f32)] * 2
        + [pltpu.VMEM((4, STEPS, 8, LANES), f32)] * 2
        + [pltpu.VMEM((2, STEPS, n_dev, 2 * CAP, LANES), f32)] * 2
        + [pltpu.VMEM((n_dev, 2 * CAP, LANES), f32)] * 2
        + [pltpu.VMEM((rows, 6 * cols), jnp.bfloat16), pltpu.VMEM((cols, 3 * rows), jnp.bfloat16)]
        + [pltpu.VMEM(source.shape, jnp.int32)] * 4
        + [pltpu.SMEM(count.shape, jnp.int32)]
        + [dma((9,)), dma((5,))]
        + [dma((4, STEPS))] * 4
        + [dma((2, STEPS))] * 2
        + [dma((2,))],
        compiler_params=pltpu.CompilerParams(
            collective_id=0, has_side_effects=True, vmem_limit_bytes=48 << 20
        ),
    )(*[pltpu.with_memory_space_constraint(x, pltpu.HBM) for x in operands], count)
    return pl.pallas_call(
        copy_out,
        out_shape=[jax.ShapeDtypeStruct(block, f32)] * 5,
        in_specs=[vmem_spec] * 5,
        out_specs=[hbm_spec] * 5,
        scratch_shapes=[dma((5,))],
    )(*[pltpu.with_memory_space_constraint(x, pltpu.VMEM) for x in results])


def solution(mesh):
    field = P(None, None, "circ", "axial")
    both = ("circ", "axial")
    return jax.shard_map(
        functools.partial(shards, mesh.shape["circ"], mesh.shape["axial"]),
        mesh=mesh,
        in_specs=(field,) * 8
        + (P(both, None), P(both, None), P(both, None, None), P(both, None), P(both)),
        out_specs=(field,) * 5,
        check_vma=False,
    )
```

```python
import functools

import jax
import jax.numpy as jnp
from jax import lax
from jax.experimental import pallas as pl
from jax.experimental.pallas import tpu as pltpu
from jax.sharding import PartitionSpec as P

STEPS = 4
CAP = 2
TIME_STEP = 0.18
MESH = pl.DeviceIdType.MESH
LANES = 128

EF, HB, AF, GB = range(4)


def pieces(x):
    high = x.astype(jnp.bfloat16)
    rest = x - high.astype(jnp.float32)
    mid = rest.astype(jnp.bfloat16)
    low = (rest - mid.astype(jnp.float32)).astype(jnp.bfloat16)
    return jnp.concatenate([high, mid, low], axis=0)


def picked_dot(matrix, x):
    return jnp.dot(matrix, pieces(x), preferred_element_type=jnp.float32)


def kernel(
    shape,
    n_circ,
    n_axial,
    e_in,
    h_in,
    a_in,
    g_in,
    ed_in,
    ec_in,
    md_in,
    mc_in,
    source_in,
    target_in,
    device_in,
    flip_in,
    count_in,
    e,
    h,
    a,
    g,
    sens,
    e_hist,
    a_hist,
    ed,
    ec,
    md,
    mc,
    row_send,
    row_recv,
    col_send,
    col_recv,
    seam_send,
    seam_recv,
    land_send,
    land_recv,
    gather_mat,
    scatter_mat,
    source_ref,
    target_ref,
    device_ref,
    flip_ref,
    count_ref,
    in_sems,
    map_sems,
    last_row_send,
    last_row_recv,
    last_col_send,
    last_col_recv,
    last_ssem,
    last_rsem,
    row_ssem,
    row_rsem,
    col_ssem,
    col_rsem,
    seam_ssem,
    seam_rsem,
    land_sems,
):
    layers, cc, ca = shape
    halves = ca // LANES
    subs = cc // 8
    n_dev = n_circ * n_axial
    rows = n_dev * CAP * 2
    cols = 2 * halves * cc
    ci = lax.axis_index("circ")
    ai = lax.axis_index("axial")
    me = ci * n_axial + ai

    barrier = pltpu.get_barrier_semaphore()
    partners = [
        (dc, da)
        for dc in reversed(range(n_circ))
        for da in reversed(range(n_axial))
        if dc or da
    ]
    far = [(dc, da) for dc, da in partners if da >= n_axial // 2]
    near = [(dc, da) for dc, da in partners if da < n_axial // 2]

    def peer_of(dc, da):
        return lax.bitwise_xor(ci, dc), lax.bitwise_xor(ai, da)

    col_recv[...] = jnp.zeros_like(col_recv)
    last_col_recv[...] = jnp.zeros_like(last_col_recv)
    for dc, da in partners:
        pl.semaphore_signal(barrier, inc=1, device_id=peer_of(dc, da), device_id_type=MESH)

    loads = [
        pltpu.make_async_copy(src, dst, in_sems.at[i])
        for i, (src, dst) in enumerate(
            [
                (e_in, e),
                (g_in, g),
                (a_in, a),
                (ed_in, ed),
                (ec_in, ec),
                (md_in, md),
                (mc_in, mc),
                (h_in, h),
                (e_in, e_hist.at[0]),
            ]
        )
    ]
    maps = [
        pltpu.make_async_copy(src, dst, map_sems.at[i])
        for i, (src, dst) in enumerate(
            [
                (source_in, source_ref),
                (target_in, target_ref),
                (device_in, device_ref),
                (flip_in, flip_ref),
                (count_in, count_ref),
            ]
        )
    ]
    for load in maps + loads:
        load.start()

    def send_all(send, recv, ssem, rsem, group):
        for dc, da in group:
            pc, pa = peer_of(dc, da)
            pltpu.make_async_remote_copy(
                src_ref=send.at[pc * n_axial + pa],
                dst_ref=recv.at[me],
                send_sem=ssem,
                recv_sem=rsem,
                device_id=(pc, pa),
                device_id_type=MESH,
            ).start()

    def keep_own(send, recv):
        recv[pl.ds(me, 1)] = send[pl.ds(me, 1)]

    def all_to_all_done(send, recv, ssem, rsem):
        return pltpu.make_async_remote_copy(
            src_ref=send.at[pl.ds(0, n_dev - 1)],
            dst_ref=recv.at[pl.ds(0, n_dev - 1)],
            send_sem=ssem,
            recv_sem=rsem,
            device_id=(ci, ai),
            device_id_type=MESH,
        )

    lane8 = lax.broadcasted_iota(jnp.int32, (8, LANES), 1)

    def row_copy(kind, t, step):
        peer = lax.rem(ci + step + n_circ, n_circ)
        return pltpu.make_async_remote_copy(
            src_ref=row_send.at[kind, t],
            dst_ref=row_recv.at[kind, t],
            send_sem=row_ssem.at[kind, t],
            recv_sem=row_rsem.at[kind, t],
            device_id=(peer, ai),
            device_id_type=MESH,
        )

    def col_copy(kind, t, step):
        peer = lax.rem(ai + step + n_axial, n_axial)
        return pltpu.make_async_remote_copy(
            src_ref=col_send.at[kind, t],
            dst_ref=col_recv.at[kind, t],
            send_sem=col_ssem.at[kind, t],
            recv_sem=col_rsem.at[kind, t],
            device_id=(ci, peer),
            device_id_type=MESH,
        )

    def pack_halos(field, kind, t, step, levels):
        edge_row = 0 if step < 0 else cc - 1
        for part, c in enumerate((0, 2)):
            for l in levels:
                at = part * layers + l
                row_send[kind, t, at : at + 1, :] = field[c, l, edge_row : edge_row + 1, :]
        col_send[kind, t] = pack_column(
            field, step, [((c * layers + l) * subs, c, l) for c in range(2) for l in levels]
        )

    def pack_column(field, step, places):
        packed = jnp.zeros((8, LANES), jnp.float32)
        for first, c, l in places:
            for s in range(subs):
                k = first + s
                lo = 0 if step < 0 else ca - LANES
                tile = field[c, l, s * 8 : s * 8 + 8, lo : lo + LANES]
                shift = k if step < 0 else (k + 1) % LANES
                if shift:
                    tile = pltpu.roll(tile, shift, 1)
                packed = jnp.where(lane8 == k, tile, packed)
        return packed

    def last_copies(q, t, step):
        row = pltpu.make_async_remote_copy(
            src_ref=last_row_send.at[q, t],
            dst_ref=last_row_recv.at[q, t],
            send_sem=last_ssem.at[q, t, 0],
            recv_sem=last_rsem.at[q, t, 0],
            device_id=(lax.rem(ci + step + n_circ, n_circ), ai),
            device_id_type=MESH,
        )
        col = pltpu.make_async_remote_copy(
            src_ref=last_col_send.at[q, t],
            dst_ref=last_col_recv.at[q, t],
            send_sem=last_ssem.at[q, t, 1],
            recv_sem=last_rsem.at[q, t, 1],
            device_id=(ci, lax.rem(ai + step + n_axial, n_axial)),
            device_id_type=MESH,
        )
        return row, col

    def pack_last(field, q, t):
        for part, c in enumerate((0, 2)):
            last_row_send[q, t, part : part + 1, :] = field[c, layers - 1, cc - 1 : cc, :]
        last_col_send[q, t] = pack_column(field, 1, [(c * subs, c, layers - 1) for c in range(2)])

    def start_last(q, t):
        row, col = last_copies(q, t, 1)
        row.start()
        pl.when(ai < n_axial - 1)(col.start)

    def wait_last(q, t):
        row, col = last_copies(q, t, 1)
        row.wait_recv()
        pl.when(ai > 0)(col.wait_recv)

    def drain_last(q, t):
        row, col = last_copies(q, t, 1)
        row.wait_send()
        pl.when(ai < n_axial - 1)(col.wait_send)

    def start_halos(kind, t, step):
        row_copy(kind, t, step).start()

        @pl.when((ai > 0) if step < 0 else (ai < n_axial - 1))
        def _():
            col_copy(kind, t, step).start()

    def wait_halos(kind, t, step):
        row_copy(kind, t, step).wait_recv()

        @pl.when((ai < n_axial - 1) if step < 0 else (ai > 0))
        def _():
            col_copy(kind, t, step).wait_recv()

    def drain_halos(kind, t, step):
        row_copy(kind, t, step).wait_send()

        @pl.when((ai > 0) if step < 0 else (ai < n_axial - 1))
        def _():
            col_copy(kind, t, step).wait_send()

    def pack_seams(field, chain, t):
        surface = jnp.concatenate(
            [
                field[c, layers - 1, :, h * LANES : (h + 1) * LANES]
                for c in (1, 2)
                for h in range(halves)
            ],
            axis=0,
        )
        ends = LANES - 1 - lax.broadcasted_iota(jnp.int32, surface.shape, 1)
        mirrored = jnp.take_along_axis(surface, ends, axis=1)
        out = picked_dot(gather_mat[...], jnp.concatenate([surface, mirrored], axis=0))
        seam_send[chain, t] = out.reshape(n_dev, 2 * CAP, LANES)

    def start_seams(chain, t, group):
        send, recv = seam_send.at[chain, t], seam_recv.at[chain, t]
        send_all(send, recv, seam_ssem.at[chain, t], seam_rsem.at[chain, t], group)
        if group is not far:
            keep_own(send, recv)

    def ghosts_of(chain, t):
        send, recv = seam_send.at[chain, t], seam_recv.at[chain, t]
        all_to_all_done(send, recv, seam_ssem.at[chain, t], seam_rsem.at[chain, t]).wait_recv()
        ghosts = picked_dot(scatter_mat[...], recv[...].reshape(rows, LANES))
        return [
            jnp.concatenate(
                [
                    ghosts[(c * halves + h) * cc : (c * halves + h + 1) * cc]
                    for h in range(halves)
                ],
                axis=1,
            )
            for c in range(2)
        ]

    sub = lax.broadcasted_iota(jnp.int32, (cc, ca), 0)
    lane = lax.broadcasted_iota(jnp.int32, (cc, ca), 1)

    def column_halo(packed, first, last):
        parts = []
        for s in range(subs):
            k = first + s
            shift = (LANES - 1 - k if last else -k) % LANES
            parts.append(pltpu.roll(packed, shift, 1) if shift else packed)
        halo = jnp.concatenate(parts, axis=0)
        return jnp.concatenate([halo] * halves, axis=1)

    def metric(diagonal, coupling, l, x, y, z):
        d0, d1, d2 = (diagonal[i, l] for i in range(3))
        o0, o1, o2 = (coupling[i, l] for i in range(3))
        return (
            d0 * x + o0 * y + o1 * z,
            o0 * x + d1 * y + o2 * z,
            o1 * x + o2 * y + d2 * z,
        )

    def forward_update(field, new, kind, chain, t, scale, levels):
        packed = col_recv[kind, t]
        for l in levels:
            v0, v1, v2 = (field[i, l] for i in range(3))
            if l + 1 < layers:
                n1, n2 = field[1, l + 1], field[2, l + 1]
            else:
                n1, n2 = ghosts_of(chain, t)

            def around(v, part):
                row = row_recv[kind, t, part * layers + l : part * layers + l + 1, :]
                return jnp.where(sub == cc - 1, row, pltpu.roll(v, cc - 1, 0)) - v

            def along(v, c):
                halo = column_halo(packed, (c * layers + l) * subs, True)
                return jnp.where(lane == ca - 1, halo, pltpu.roll(v, ca - 1, 1)) - v

            x = around(v2, 1) - along(v1, 1)
            y = along(v0, 0) - (n2 - v2)
            z = (n1 - v1) - around(v0, 0)
            change = metric(md, mc, l, x, y, z)
            for i in range(3):
                new[i, l] = new[i, l] + scale * change[i]

    def backward_update(field, new, kept, kind, t, scale, levels):
        packed = col_recv[kind, t]
        packed_last = last_col_recv[kind // 2, t]
        for l in levels:
            v0, v1, v2 = (field[i, l] for i in range(3))

            def around(v, part):
                if l == layers - 1:
                    row = last_row_recv[kind // 2, t, part : part + 1, :]
                else:
                    row = row_recv[kind, t, part * layers + l : part * layers + l + 1, :]
                return v - jnp.where(sub == 0, row, pltpu.roll(v, 1, 0))

            def along(v, c):
                if l == layers - 1:
                    halo = column_halo(packed_last, c * subs, False)
                else:
                    halo = column_halo(packed, (c * layers + l) * subs, False)
                return v - jnp.where(lane == 0, halo, pltpu.roll(v, 1, 1))

            r1 = v1 - field[1, l - 1] if l else v1
            r2 = v2 - field[2, l - 1] if l else v2
            x = around(v2, 1) - along(v1, 1)
            y = along(v0, 0) - r2
            z = r1 - around(v0, 0)
            change = metric(ed, ec, l, x, y, z)
            for i in range(3):
                value = new[i, l] + scale * change[i]
                new[i, l] = value
                if kept is not None:
                    kept[i, l] = value

    seams = source_ref.shape[1]
    for load in maps:
        load.wait()
    device = device_ref[...]
    count = count_ref[0]
    slot_row = lax.broadcasted_iota(jnp.int32, (1, seams), 1)
    si = lax.broadcasted_iota(jnp.int32, (seams, seams), 0)
    sj = lax.broadcasted_iota(jnp.int32, (seams, seams), 1)
    device_f = device.astype(jnp.float32)
    device_col = jnp.sum(
        jnp.where(si == sj, jnp.broadcast_to(device_f, (seams, seams)), 0.0), axis=1, keepdims=True
    )
    earlier = (device_col == device_f) & (si < sj)
    rank = jnp.sum(jnp.where(earlier, 1.0, 0.0), axis=0, keepdims=True)
    code = jnp.where(slot_row < count, device_f * CAP + rank, -1.0)
    ri = lax.broadcasted_iota(jnp.int32, (rows, seams), 0)
    place = lax.div(ri, 2).astype(jnp.float32) == code

    def picked(values):
        return jnp.sum(
            jnp.where(place, values.astype(jnp.float32), 0.0), axis=1, keepdims=True
        ).astype(jnp.int32)

    comp = lax.rem(lax.broadcasted_iota(jnp.int32, (rows, 1), 0), 2)

    def column_of(block):
        return (comp * halves + lax.rem(block, halves)) * cc + lax.div(block, halves)

    valid = jnp.sum(jnp.where(place, 1.0, 0.0), axis=1, keepdims=True) > 0.5
    landing = jnp.where(valid, column_of(picked(target_ref[...])), -1).astype(jnp.float32)
    group_lane = lax.broadcasted_iota(jnp.int32, (rows, LANES), 1)
    own_lane = group_lane == lax.rem(lax.broadcasted_iota(jnp.int32, (rows, LANES), 0), 2 * CAP)
    spots = jnp.where(own_lane, landing, 0.0).reshape(n_dev, 2 * CAP, LANES)
    land_send[...] = jnp.sum(spots, axis=1, keepdims=True)
    flipped = picked(flip_ref[...]) == 1
    src_col = jnp.where(valid, column_of(picked(source_ref[...])) + jnp.where(flipped, cols, 0), -1)
    sign = jnp.where(flipped & (comp == 1), -1.0, 1.0)
    ki = lax.broadcasted_iota(jnp.int32, (rows, 2 * cols), 1)
    gather = jnp.where(ki == src_col, sign, 0.0).astype(jnp.bfloat16)
    gather_mat[...] = jnp.concatenate([gather] * 3, axis=1)

    inner, last = list(range(layers - 1)), [layers - 1]
    loads[0].wait()
    pack_seams(e, 0, 0)
    pack_halos(e, EF, 0, -1, inner + last)
    loads[1].wait()
    pack_halos(g, GB, 0, 1, inner)
    pack_last(g, 1, 0)
    pl.semaphore_wait(barrier, n_dev - 1)
    start_last(1, 0)
    start_halos(GB, 0, 1)
    start_halos(EF, 0, -1)
    send_all(land_send, land_recv, land_sems.at[0], land_sems.at[1], partners)
    keep_own(land_send, land_recv)
    start_seams(0, 0, partners)
    for load in loads[2:]:
        load.wait()

    def step(t, carry):
        wait_last(1, t)
        backward_update(g, a, a_hist.at[STEPS - 1 - t], GB, t, -TIME_STEP, last)
        pack_seams(a, 1, t)
        start_seams(1, t, partners)
        wait_halos(GB, t, 1)
        backward_update(g, a, a_hist.at[STEPS - 1 - t], GB, t, -TIME_STEP, inner)
        pack_halos(a, AF, t, -1, inner + last)
        start_halos(AF, t, -1)

        @pl.when(t == 0)
        def _():
            all_to_all_done(land_send, land_recv, land_sems.at[0], land_sems.at[1]).wait_recv()
            came = jnp.broadcast_to(land_recv[...], (n_dev, 2 * CAP, LANES)).reshape(rows, LANES)
            spot = jnp.sum(jnp.where(own_lane, came, 0.0), axis=1, keepdims=True)
            spread = jnp.where(spot == group_lane.astype(jnp.float32), 1.0, 0.0)
            scatter = spread.T[:cols].astype(jnp.bfloat16)
            scatter_mat[...] = jnp.concatenate([scatter] * 3, axis=1)

        wait_halos(EF, t, -1)
        forward_update(e, h, EF, 0, t, -TIME_STEP, inner)
        pack_halos(h, HB, t, 1, inner)
        start_halos(HB, t, 1)
        forward_update(e, h, EF, 0, t, -TIME_STEP, last)
        pack_last(h, 0, t)
        start_last(0, t)

        @pl.when(t == STEPS - 1)
        def _():
            for l in range(layers):
                for i in range(3):
                    total = e_hist[STEPS - 1, i, l] * a_hist[STEPS - 1, i, l]
                    for n in reversed(range(STEPS - 1)):
                        total = total + e_hist[n, i, l] * a_hist[n, i, l]
                    sens[i, l] = total

        wait_halos(AF, t, -1)
        forward_update(a, g, AF, 1, t, TIME_STEP, inner)

        @pl.when(t + 1 < STEPS)
        def _():
            pack_halos(g, GB, t + 1, 1, inner)
            start_halos(GB, t + 1, 1)

        forward_update(a, g, AF, 1, t, TIME_STEP, last)

        @pl.when(t + 1 < STEPS)
        def _():
            pack_last(g, 1, t + 1)
            start_last(1, t + 1)
            wait_last(0, t)
            backward_update(h, e, e_hist.at[t + 1], HB, t, TIME_STEP, last)
            pack_seams(e, 0, t + 1)
            start_seams(0, t + 1, partners)
            wait_halos(HB, t, 1)
            backward_update(h, e, e_hist.at[t + 1], HB, t, TIME_STEP, inner)
            pack_halos(e, EF, t + 1, -1, inner + last)
            start_halos(EF, t + 1, -1)

        return carry

    lax.fori_loop(0, STEPS, step, 0)

    def drain(t, carry):
        for kind, way in ((EF, -1), (HB, 1), (AF, -1), (GB, 1)):
            drain_halos(kind, t, way)
        drain_last(1, t)
        for chain in range(2):
            all_to_all_done(
                seam_send.at[chain, t],
                seam_recv.at[chain, t],
                seam_ssem.at[chain, t],
                seam_rsem.at[chain, t],
            ).wait_send()
        return carry

    lax.fori_loop(0, STEPS, drain, 0)
    all_to_all_done(land_send, land_recv, land_sems.at[0], land_sems.at[1]).wait_send()
    wait_halos(HB, STEPS - 1, 1)
    wait_last(0, STEPS - 1)
    backward_update(h, e, None, HB, STEPS - 1, TIME_STEP, inner + last)
    for t in range(STEPS):
        drain_last(0, t)


def copy_out(*refs):
    sources, targets, sems = refs[:5], refs[5:10], refs[10]
    stores = [
        pltpu.make_async_copy(src, dst, sems.at[i])
        for i, (src, dst) in enumerate(zip(sources, targets))
    ]
    for store in stores:
        store.start()
    for store in stores:
        store.wait()


def shards(n_circ, n_axial, *args):
    fields, (source, target, device, flip, count) = args[:8], args[8:]
    block = fields[0].shape
    layers, cc, ca = block[1:]
    n_dev = n_circ * n_axial
    rows = n_dev * CAP * 2
    cols = 2 * (ca // LANES) * cc
    operands = [*fields, source, target, device.reshape(1, -1), flip]
    f32 = jnp.float32
    dma = pltpu.SemaphoreType.DMA
    hbm_spec = pl.BlockSpec(memory_space=pltpu.HBM)
    vmem_spec = pl.BlockSpec(memory_space=pltpu.VMEM)
    results = pl.pallas_call(
        functools.partial(kernel, (layers, cc, ca), n_circ, n_axial),
        out_shape=[pltpu.VMEM(block, f32)] * 5,
        in_specs=[hbm_spec] * 12 + [pl.BlockSpec(memory_space=pl.ANY)],
        out_specs=[vmem_spec] * 5,
        scratch_shapes= [pltpu.VMEM((STEPS,) + block, f32)] * 2
        + [pltpu.VMEM(block, f32)] * 4
        + [pltpu.VMEM((4, STEPS, 2 * layers, ca), f32)] * 2
        + [pltpu.VMEM((4, STEPS, 8, LANES), f32)] * 2
        + [pltpu.VMEM((2, STEPS, n_dev, 2 * CAP, LANES), f32)] * 2
        + [pltpu.VMEM((n_dev, 1, LANES), f32)] * 2
        + [pltpu.VMEM((rows, 6 * cols), jnp.bfloat16), pltpu.VMEM((cols, 3 * rows), jnp.bfloat16)]
        + [pltpu.VMEM(source.shape, jnp.int32)] * 4
        + [pltpu.SMEM(count.shape, jnp.int32)]
        + [dma((9,)), dma((5,))]
        + [pltpu.VMEM((2, STEPS, 2, ca), f32)] * 2
        + [pltpu.VMEM((2, STEPS, 8, LANES), f32)] * 2
        + [dma((2, STEPS, 2))] * 2
        + [dma((4, STEPS))] * 4
        + [dma((2, STEPS))] * 2
        + [dma((2,))],
        compiler_params=pltpu.CompilerParams(
            collective_id=0, has_side_effects=True, vmem_limit_bytes=48 << 20
        ),
    )(*[pltpu.with_memory_space_constraint(x, pltpu.HBM) for x in operands], count)
    return pl.pallas_call(
        copy_out,
        out_shape=[jax.ShapeDtypeStruct(block, f32)] * 5,
        in_specs=[vmem_spec] * 5,
        out_specs=[hbm_spec] * 5,
        scratch_shapes=[dma((5,))],
    )(*[pltpu.with_memory_space_constraint(x, pltpu.VMEM) for x in results])


def solution(mesh):
    field = P(None, None, "circ", "axial")
    both = ("circ", "axial")
    return jax.shard_map(
        functools.partial(shards, mesh.shape["circ"], mesh.shape["axial"]),
        mesh=mesh,
        in_specs=(field,) * 8
        + (P(both, None), P(both, None), P(both, None, None), P(both, None), P(both)),
        out_specs=(field,) * 5,
        check_vma=False,
    )
```

```python
import functools

import jax
import jax.numpy as jnp
from jax import lax
from jax.experimental import pallas as pl
from jax.experimental.pallas import tpu as pltpu
from jax.sharding import PartitionSpec as P

STEPS = 4
CAP = 2
TIME_STEP = 0.18
MESH = pl.DeviceIdType.MESH
LANES = 128

EF, HB, AF, GB = range(4)


def pieces(x):
    high = x.astype(jnp.bfloat16)
    rest = x - high.astype(jnp.float32)
    mid = rest.astype(jnp.bfloat16)
    low = (rest - mid.astype(jnp.float32)).astype(jnp.bfloat16)
    return jnp.concatenate([high, mid, low], axis=0)


def picked_dot(matrix, x):
    return jnp.dot(matrix, pieces(x), preferred_element_type=jnp.float32)


def kernel(
    shape,
    n_circ,
    n_axial,
    e_in,
    h_in,
    a_in,
    g_in,
    ed_in,
    ec_in,
    md_in,
    mc_in,
    source_in,
    target_in,
    device_in,
    flip_in,
    count_in,
    e,
    h,
    a,
    g,
    sens,
    e_hist,
    a_hist,
    ed,
    ec,
    md,
    mc,
    row_send,
    row_recv,
    col_send,
    col_recv,
    seam_send,
    seam_recv,
    land_send,
    land_recv,
    table,
    entry_row,
    entry_ref,
    entry_sem,
    scatter_mat,
    source_ref,
    target_ref,
    device_ref,
    flip_ref,
    count_ref,
    in_sems,
    map_sems,
    last_row_send,
    last_row_recv,
    last_col_send,
    last_col_recv,
    last_ssem,
    last_rsem,
    row_ssem,
    row_rsem,
    col_ssem,
    col_rsem,
    seam_ssem,
    seam_rsem,
    land_sems,
):
    layers, cc, ca = shape
    halves = ca // LANES
    subs = cc // 8
    n_dev = n_circ * n_axial
    rows = n_dev * CAP * 2
    cols = 2 * halves * cc
    blocks = halves * cc
    ci = lax.axis_index("circ")
    ai = lax.axis_index("axial")
    me = ci * n_axial + ai

    barrier = pltpu.get_barrier_semaphore()
    partners = [
        (dc, da)
        for dc in reversed(range(n_circ))
        for da in reversed(range(n_axial))
        if dc or da
    ]
    def peer_of(dc, da):
        return lax.bitwise_xor(ci, dc), lax.bitwise_xor(ai, da)

    col_recv[...] = jnp.zeros_like(col_recv)
    last_col_recv[...] = jnp.zeros_like(last_col_recv)
    for dc, da in partners:
        pl.semaphore_signal(barrier, inc=1, device_id=peer_of(dc, da), device_id_type=MESH)

    loads = [
        pltpu.make_async_copy(src, dst, in_sems.at[i])
        for i, (src, dst) in enumerate(
            [
                (e_in, e),
                (g_in, g),
                (a_in, a),
                (ed_in, ed),
                (ec_in, ec),
                (md_in, md),
                (mc_in, mc),
                (h_in, h),
                (e_in, e_hist.at[0]),
            ]
        )
    ]
    maps = [
        pltpu.make_async_copy(src, dst, map_sems.at[i])
        for i, (src, dst) in enumerate(
            [
                (source_in, source_ref),
                (target_in, target_ref),
                (device_in, device_ref),
                (flip_in, flip_ref),
                (count_in, count_ref),
            ]
        )
    ]
    for load in maps + loads:
        load.start()

    def send_all(send, recv, ssem, rsem, group):
        for dc, da in group:
            pc, pa = peer_of(dc, da)
            pltpu.make_async_remote_copy(
                src_ref=send.at[pc * n_axial + pa],
                dst_ref=recv.at[me],
                send_sem=ssem,
                recv_sem=rsem,
                device_id=(pc, pa),
                device_id_type=MESH,
            ).start()

    def keep_own(send, recv):
        recv[pl.ds(me, 1)] = send[pl.ds(me, 1)]

    def all_to_all_done(send, recv, ssem, rsem):
        return pltpu.make_async_remote_copy(
            src_ref=send.at[pl.ds(0, n_dev - 1)],
            dst_ref=recv.at[pl.ds(0, n_dev - 1)],
            send_sem=ssem,
            recv_sem=rsem,
            device_id=(ci, ai),
            device_id_type=MESH,
        )

    lane8 = lax.broadcasted_iota(jnp.int32, (8, LANES), 1)

    def row_copy(kind, t, step):
        peer = lax.rem(ci + step + n_circ, n_circ)
        return pltpu.make_async_remote_copy(
            src_ref=row_send.at[kind, t],
            dst_ref=row_recv.at[kind, t],
            send_sem=row_ssem.at[kind, t],
            recv_sem=row_rsem.at[kind, t],
            device_id=(peer, ai),
            device_id_type=MESH,
        )

    def col_copy(kind, t, step):
        peer = lax.rem(ai + step + n_axial, n_axial)
        return pltpu.make_async_remote_copy(
            src_ref=col_send.at[kind, t],
            dst_ref=col_recv.at[kind, t],
            send_sem=col_ssem.at[kind, t],
            recv_sem=col_rsem.at[kind, t],
            device_id=(ci, peer),
            device_id_type=MESH,
        )

    def pack_halos(field, kind, t, step, levels):
        edge_row = 0 if step < 0 else cc - 1
        for part, c in enumerate((0, 2)):
            for l in levels:
                at = part * layers + l
                row_send[kind, t, at : at + 1, :] = field[c, l, edge_row : edge_row + 1, :]
        col_send[kind, t] = pack_column(
            field, step, [((c * layers + l) * subs, c, l) for c in range(2) for l in levels]
        )

    def pack_column(field, step, places):
        packed = jnp.zeros((8, LANES), jnp.float32)
        for first, c, l in places:
            for s in range(subs):
                k = first + s
                lo = 0 if step < 0 else ca - LANES
                tile = field[c, l, s * 8 : s * 8 + 8, lo : lo + LANES]
                shift = k if step < 0 else (k + 1) % LANES
                if shift:
                    tile = pltpu.roll(tile, shift, 1)
                packed = jnp.where(lane8 == k, tile, packed)
        return packed

    def last_copies(q, t, step):
        row = pltpu.make_async_remote_copy(
            src_ref=last_row_send.at[q, t],
            dst_ref=last_row_recv.at[q, t],
            send_sem=last_ssem.at[q, t, 0],
            recv_sem=last_rsem.at[q, t, 0],
            device_id=(lax.rem(ci + step + n_circ, n_circ), ai),
            device_id_type=MESH,
        )
        col = pltpu.make_async_remote_copy(
            src_ref=last_col_send.at[q, t],
            dst_ref=last_col_recv.at[q, t],
            send_sem=last_ssem.at[q, t, 1],
            recv_sem=last_rsem.at[q, t, 1],
            device_id=(ci, lax.rem(ai + step + n_axial, n_axial)),
            device_id_type=MESH,
        )
        return row, col

    def pack_last(field, q, t):
        for part, c in enumerate((0, 2)):
            last_row_send[q, t, part : part + 1, :] = field[c, layers - 1, cc - 1 : cc, :]
        last_col_send[q, t] = pack_column(field, 1, [(c * subs, c, layers - 1) for c in range(2)])

    def start_last(q, t):
        row, col = last_copies(q, t, 1)
        row.start()
        pl.when(ai < n_axial - 1)(col.start)

    def wait_last(q, t):
        row, col = last_copies(q, t, 1)
        row.wait_recv()
        pl.when(ai > 0)(col.wait_recv)

    def drain_last(q, t):
        row, col = last_copies(q, t, 1)
        row.wait_send()
        pl.when(ai < n_axial - 1)(col.wait_send)

    def start_halos(kind, t, step):
        row_copy(kind, t, step).start()

        @pl.when((ai > 0) if step < 0 else (ai < n_axial - 1))
        def _():
            col_copy(kind, t, step).start()

    def wait_halos(kind, t, step):
        row_copy(kind, t, step).wait_recv()

        @pl.when((ai < n_axial - 1) if step < 0 else (ai > 0))
        def _():
            col_copy(kind, t, step).wait_recv()

    def drain_halos(kind, t, step):
        row_copy(kind, t, step).wait_send()

        @pl.when((ai > 0) if step < 0 else (ai < n_axial - 1))
        def _():
            col_copy(kind, t, step).wait_send()

    def fill_table(field):
        ends = LANES - 1 - lax.broadcasted_iota(jnp.int32, (cc, LANES), 1)
        for c in (1, 2):
            for h in range(halves):
                face = field[c, layers - 1, :, h * LANES : (h + 1) * LANES]
                turned = jnp.take_along_axis(face, ends, axis=1)
                at = 2 * h + c - 1
                table[pl.ds(at, cc, stride=2 * halves), :] = face
                table[pl.ds(2 * blocks + at, cc, stride=2 * halves), :] = -turned if c == 2 else turned

    def rows_of(peer, slot):
        entry = jnp.clip(entry_ref[0, peer * CAP + slot], 0, 2 * blocks)
        return table[pl.ds(2 * entry, 2), :]

    def send_seams(chain, t):
        send, recv = seam_send.at[chain, t], seam_recv.at[chain, t]
        for dc, da in partners:
            pc, pa = peer_of(dc, da)
            peer = pc * n_axial + pa
            for slot in range(CAP):
                send[peer, 2 * slot : 2 * slot + 2] = rows_of(peer, slot)
            pltpu.make_async_remote_copy(
                src_ref=send.at[peer],
                dst_ref=recv.at[me],
                send_sem=seam_ssem.at[chain, t],
                recv_sem=seam_rsem.at[chain, t],
                device_id=(pc, pa),
                device_id_type=MESH,
            ).start()
        for slot in range(CAP):
            recv[me, 2 * slot : 2 * slot + 2] = rows_of(me, slot)

    def ghosts_of(chain, t):
        send, recv = seam_send.at[chain, t], seam_recv.at[chain, t]
        all_to_all_done(send, recv, seam_ssem.at[chain, t], seam_rsem.at[chain, t]).wait_recv()
        ghosts = picked_dot(scatter_mat[...], recv[...].reshape(rows, LANES))
        return [
            jnp.concatenate(
                [
                    ghosts[(c * halves + h) * cc : (c * halves + h + 1) * cc]
                    for h in range(halves)
                ],
                axis=1,
            )
            for c in range(2)
        ]

    sub = lax.broadcasted_iota(jnp.int32, (cc, ca), 0)
    lane = lax.broadcasted_iota(jnp.int32, (cc, ca), 1)

    def column_halo(packed, first, last):
        parts = []
        for s in range(subs):
            k = first + s
            shift = (LANES - 1 - k if last else -k) % LANES
            parts.append(pltpu.roll(packed, shift, 1) if shift else packed)
        halo = jnp.concatenate(parts, axis=0)
        return jnp.concatenate([halo] * halves, axis=1)

    def metric(diagonal, coupling, l, x, y, z):
        d0, d1, d2 = (diagonal[i, l] for i in range(3))
        o0, o1, o2 = (coupling[i, l] for i in range(3))
        return (
            d0 * x + o0 * y + o1 * z,
            o0 * x + d1 * y + o2 * z,
            o1 * x + o2 * y + d2 * z,
        )

    def forward_update(field, new, kind, t, scale, levels):
        packed = col_recv[kind, t]
        for l in levels:
            v0, v1, v2 = (field[i, l] for i in range(3))
            inside = l + 1 < layers
            r1 = (field[1, l + 1] if inside else 0.0) - v1
            r2 = (field[2, l + 1] if inside else 0.0) - v2

            def around(v, part):
                row = row_recv[kind, t, part * layers + l : part * layers + l + 1, :]
                return jnp.where(sub == cc - 1, row, pltpu.roll(v, cc - 1, 0)) - v

            def along(v, c):
                halo = column_halo(packed, (c * layers + l) * subs, True)
                return jnp.where(lane == ca - 1, halo, pltpu.roll(v, ca - 1, 1)) - v

            x = around(v2, 1) - along(v1, 1)
            y = along(v0, 0) - r2
            z = r1 - around(v0, 0)
            change = metric(md, mc, l, x, y, z)
            for i in range(3):
                new[i, l] = new[i, l] + scale * change[i]

    def add_rim(new, chain, t, scale):
        g0, g1 = ghosts_of(chain, t)
        change = metric(md, mc, layers - 1, 0.0, -g1, g0)
        for i in range(3):
            new[i, layers - 1] = new[i, layers - 1] + scale * change[i]

    def backward_update(field, new, kept, kind, t, scale, levels):
        packed = col_recv[kind, t]
        for l in levels:
            v0, v1, v2 = (field[i, l] for i in range(3))

            def around(v, part):
                if l == layers - 1:
                    return v - jnp.where(sub == 0, 0.0, pltpu.roll(v, 1, 0))
                row = row_recv[kind, t, part * layers + l : part * layers + l + 1, :]
                return v - jnp.where(sub == 0, row, pltpu.roll(v, 1, 0))

            def along(v, c):
                if l == layers - 1:
                    return v - jnp.where(lane == 0, 0.0, pltpu.roll(v, 1, 1))
                halo = column_halo(packed, (c * layers + l) * subs, False)
                return v - jnp.where(lane == 0, halo, pltpu.roll(v, 1, 1))

            r1 = v1 - field[1, l - 1] if l else v1
            r2 = v2 - field[2, l - 1] if l else v2
            x = around(v2, 1) - along(v1, 1)
            y = along(v0, 0) - r2
            z = r1 - around(v0, 0)
            change = metric(ed, ec, l, x, y, z)
            for i in range(3):
                value = new[i, l] + scale * change[i]
                new[i, l] = value
                if kept is not None:
                    kept[i, l] = value

    def add_halo(new, kept, q, t, scale):
        packed = last_col_recv[q, t]
        row0, row2 = (
            jnp.where(sub == 0, last_row_recv[q, t, part : part + 1, :], 0.0) for part in range(2)
        )
        col0, col1 = (
            jnp.where(lane == 0, column_halo(packed, c * subs, False), 0.0) for c in range(2)
        )
        change = metric(ed, ec, layers - 1, col1 - row2, -col0, row0)
        for i in range(3):
            value = new[i, layers - 1] + scale * change[i]
            new[i, layers - 1] = value
            if kept is not None:
                kept[i, layers - 1] = value

    seams = source_ref.shape[1]
    for load in maps:
        load.wait()
    device = device_ref[...]
    count = count_ref[0]
    slot_row = lax.broadcasted_iota(jnp.int32, (1, seams), 1)
    si = lax.broadcasted_iota(jnp.int32, (seams, seams), 0)
    sj = lax.broadcasted_iota(jnp.int32, (seams, seams), 1)
    device_f = device.astype(jnp.float32)
    device_col = jnp.sum(
        jnp.where(si == sj, jnp.broadcast_to(device_f, (seams, seams)), 0.0), axis=1, keepdims=True
    )
    earlier = (device_col == device_f) & (si < sj)
    rank = jnp.sum(jnp.where(earlier, 1.0, 0.0), axis=0, keepdims=True)
    code = jnp.where(slot_row < count, device_f * CAP + rank, -1.0)
    ri = lax.broadcasted_iota(jnp.int32, (rows, seams), 0)
    place = lax.div(ri, 2).astype(jnp.float32) == code

    def picked(values):
        return jnp.sum(
            jnp.where(place, values.astype(jnp.float32), 0.0), axis=1, keepdims=True
        ).astype(jnp.int32)

    comp = lax.rem(lax.broadcasted_iota(jnp.int32, (rows, 1), 0), 2)

    def column_of(block):
        return (comp * halves + lax.rem(block, halves)) * cc + lax.div(block, halves)

    valid = jnp.sum(jnp.where(place, 1.0, 0.0), axis=1, keepdims=True) > 0.5
    landing = jnp.where(valid, column_of(picked(target_ref[...])), -1).astype(jnp.float32)
    group_lane = lax.broadcasted_iota(jnp.int32, (rows, LANES), 1)
    own_lane = group_lane == lax.rem(lax.broadcasted_iota(jnp.int32, (rows, LANES), 0), 2 * CAP)
    spots = jnp.where(own_lane, landing, 0.0).reshape(n_dev, 2 * CAP, LANES)
    land_send[...] = jnp.sum(spots, axis=1, keepdims=True)

    def upright(row):
        spread = jnp.broadcast_to(row.astype(jnp.float32), (seams, seams))
        return jnp.sum(jnp.where(si == sj, spread, 0.0), axis=1, keepdims=True)

    width = entry_row.shape[1]
    slot_lane = lax.broadcasted_iota(jnp.int32, (seams, width), 1).astype(jnp.float32)
    aimed = slot_lane == upright(code)
    taken = upright(source_ref[...] + blocks * flip_ref[...])
    entry = jnp.sum(jnp.where(aimed, taken, 0.0), axis=0, keepdims=True)
    live = jnp.sum(jnp.where(aimed, 1.0, 0.0), axis=0, keepdims=True) > 0.5
    entry_row[...] = jnp.where(live, entry, 2.0 * blocks).astype(jnp.int32)
    entries = pltpu.make_async_copy(entry_row, entry_ref, entry_sem.at[0])
    entries.start()
    table[pl.ds(4 * blocks, 8), :] = jnp.zeros((8, LANES), jnp.float32)

    inner, last = list(range(layers - 1)), [layers - 1]
    loads[0].wait()
    fill_table(e)
    entries.wait()
    pack_halos(e, EF, 0, -1, inner + last)
    loads[1].wait()
    pack_halos(g, GB, 0, 1, inner)
    pack_last(g, 1, 0)
    pl.semaphore_wait(barrier, n_dev - 1)
    start_last(1, 0)
    start_halos(GB, 0, 1)
    start_halos(EF, 0, -1)
    for partner in partners:
        send_all(land_send, land_recv, land_sems.at[0], land_sems.at[1], [partner])
    send_seams(0, 0)
    keep_own(land_send, land_recv)
    for load in loads[2:]:
        load.wait()
    backward_update(g, a, None, GB, 0, -TIME_STEP, last)

    def step(t, carry):
        wait_last(1, t)
        add_halo(a, a_hist.at[STEPS - 1 - t], 1, t, -TIME_STEP)
        fill_table(a)
        send_seams(1, t)
        wait_halos(GB, t, 1)
        backward_update(g, a, a_hist.at[STEPS - 1 - t], GB, t, -TIME_STEP, inner)
        pack_halos(a, AF, t, -1, inner + last)
        start_halos(AF, t, -1)

        @pl.when(t == 0)
        def _():
            all_to_all_done(land_send, land_recv, land_sems.at[0], land_sems.at[1]).wait_recv()
            came = jnp.broadcast_to(land_recv[...], (n_dev, 2 * CAP, LANES)).reshape(rows, LANES)
            spot = jnp.sum(jnp.where(own_lane, came, 0.0), axis=1, keepdims=True)
            spread = jnp.where(spot == group_lane.astype(jnp.float32), 1.0, 0.0)
            scatter = spread.T[:cols].astype(jnp.bfloat16)
            scatter_mat[...] = jnp.concatenate([scatter] * 3, axis=1)

        wait_halos(EF, t, -1)
        forward_update(e, h, EF, t, -TIME_STEP, inner + last)
        pack_halos(h, HB, t, 1, inner)
        start_halos(HB, t, 1)
        add_rim(h, 0, t, -TIME_STEP)
        pack_last(h, 0, t)
        start_last(0, t)
        backward_update(h, e, None, HB, t, TIME_STEP, last)

        @pl.when(t == STEPS - 1)
        def _():
            for l in range(layers):
                for i in range(3):
                    total = e_hist[STEPS - 1, i, l] * a_hist[STEPS - 1, i, l]
                    for n in reversed(range(STEPS - 1)):
                        total = total + e_hist[n, i, l] * a_hist[n, i, l]
                    sens[i, l] = total

        wait_halos(AF, t, -1)
        forward_update(a, g, AF, t, TIME_STEP, inner + last)

        @pl.when(t + 1 < STEPS)
        def _():
            pack_halos(g, GB, t + 1, 1, inner)
            start_halos(GB, t + 1, 1)

        add_rim(g, 1, t, TIME_STEP)

        @pl.when(t + 1 < STEPS)
        def _():
            pack_last(g, 1, t + 1)
            start_last(1, t + 1)
            backward_update(g, a, None, GB, t, -TIME_STEP, last)
            wait_last(0, t)
            add_halo(e, e_hist.at[t + 1], 0, t, TIME_STEP)
            fill_table(e)
            send_seams(0, t + 1)
            wait_halos(HB, t, 1)
            backward_update(h, e, e_hist.at[t + 1], HB, t, TIME_STEP, inner)
            pack_halos(e, EF, t + 1, -1, inner + last)
            start_halos(EF, t + 1, -1)

        return carry

    lax.fori_loop(0, STEPS, step, 0)

    def drain(t, carry):
        for kind, way in ((EF, -1), (HB, 1), (AF, -1), (GB, 1)):
            drain_halos(kind, t, way)
        drain_last(1, t)
        for chain in range(2):
            all_to_all_done(
                seam_send.at[chain, t],
                seam_recv.at[chain, t],
                seam_ssem.at[chain, t],
                seam_rsem.at[chain, t],
            ).wait_send()
        return carry

    lax.fori_loop(0, STEPS, drain, 0)
    all_to_all_done(land_send, land_recv, land_sems.at[0], land_sems.at[1]).wait_send()
    wait_halos(HB, STEPS - 1, 1)
    backward_update(h, e, None, HB, STEPS - 1, TIME_STEP, inner)
    wait_last(0, STEPS - 1)
    add_halo(e, None, 0, STEPS - 1, TIME_STEP)
    for t in range(STEPS):
        drain_last(0, t)


def copy_out(*refs):
    sources, targets, sems = refs[:5], refs[5:10], refs[10]
    stores = [
        pltpu.make_async_copy(src, dst, sems.at[i])
        for i, (src, dst) in enumerate(zip(sources, targets))
    ]
    for store in stores:
        store.start()
    for store in stores:
        store.wait()


def shards(n_circ, n_axial, *args):
    fields, (source, target, device, flip, count) = args[:8], args[8:]
    block = fields[0].shape
    layers, cc, ca = block[1:]
    n_dev = n_circ * n_axial
    rows = n_dev * CAP * 2
    cols = 2 * (ca // LANES) * cc
    width = -(-n_dev * CAP // LANES) * LANES
    operands = [*fields, source, target, device.reshape(1, -1), flip]
    f32 = jnp.float32
    dma = pltpu.SemaphoreType.DMA
    hbm_spec = pl.BlockSpec(memory_space=pltpu.HBM)
    vmem_spec = pl.BlockSpec(memory_space=pltpu.VMEM)
    results = pl.pallas_call(
        functools.partial(kernel, (layers, cc, ca), n_circ, n_axial),
        out_shape=[pltpu.VMEM(block, f32)] * 5,
        in_specs=[hbm_spec] * 12 + [pl.BlockSpec(memory_space=pl.ANY)],
        out_specs=[vmem_spec] * 5,
        scratch_shapes= [pltpu.VMEM((STEPS,) + block, f32)] * 2
        + [pltpu.VMEM(block, f32)] * 4
        + [pltpu.VMEM((4, STEPS, 2 * layers, ca), f32)] * 2
        + [pltpu.VMEM((4, STEPS, 8, LANES), f32)] * 2
        + [pltpu.VMEM((2, STEPS, n_dev, 2 * CAP, LANES), f32)] * 2
        + [pltpu.VMEM((n_dev, 1, LANES), f32)] * 2
        + [pltpu.VMEM((4 * (ca // LANES) * cc + 8, LANES), f32)]
        + [pltpu.VMEM((1, width), jnp.int32), pltpu.SMEM((1, width), jnp.int32), dma((1,))]
        + [pltpu.VMEM((cols, 3 * rows), jnp.bfloat16)]
        + [pltpu.VMEM(source.shape, jnp.int32)] * 4
        + [pltpu.SMEM(count.shape, jnp.int32)]
        + [dma((9,)), dma((5,))]
        + [pltpu.VMEM((2, STEPS, 2, ca), f32)] * 2
        + [pltpu.VMEM((2, STEPS, 8, LANES), f32)] * 2
        + [dma((2, STEPS, 2))] * 2
        + [dma((4, STEPS))] * 4
        + [dma((2, STEPS))] * 2
        + [dma((2,))],
        compiler_params=pltpu.CompilerParams(
            collective_id=0, has_side_effects=True, vmem_limit_bytes=48 << 20
        ),
    )(*[pltpu.with_memory_space_constraint(x, pltpu.HBM) for x in operands], count)
    return pl.pallas_call(
        copy_out,
        out_shape=[jax.ShapeDtypeStruct(block, f32)] * 5,
        in_specs=[vmem_spec] * 5,
        out_specs=[hbm_spec] * 5,
        scratch_shapes=[dma((5,))],
    )(*[pltpu.with_memory_space_constraint(x, pltpu.VMEM) for x in results])


def solution(mesh):
    field = P(None, None, "circ", "axial")
    both = ("circ", "axial")
    return jax.shard_map(
        functools.partial(shards, mesh.shape["circ"], mesh.shape["axial"]),
        mesh=mesh,
        in_specs=(field,) * 8
        + (P(both, None), P(both, None), P(both, None, None), P(both, None), P(both)),
        out_specs=(field,) * 5,
        check_vma=False,
    )
```

```python
import functools

import jax
import jax.numpy as jnp
from jax import lax
from jax.experimental import pallas as pl
from jax.experimental.pallas import tpu as pltpu
from jax.sharding import PartitionSpec as P

STEPS = 4
CAP = 2
TIME_STEP = 0.18
MESH = pl.DeviceIdType.MESH
LANES = 128

EF, HB, AF, GB = range(4)


def pieces(x):
    high = x.astype(jnp.bfloat16)
    rest = x - high.astype(jnp.float32)
    mid = rest.astype(jnp.bfloat16)
    low = (rest - mid.astype(jnp.float32)).astype(jnp.bfloat16)
    return jnp.concatenate([high, mid, low], axis=0)


def picked_dot(matrix, x):
    return jnp.dot(matrix, pieces(x), preferred_element_type=jnp.float32)


def kernel(
    shape,
    n_circ,
    n_axial,
    e_in,
    h_in,
    a_in,
    g_in,
    ed_in,
    ec_in,
    md_in,
    mc_in,
    source_in,
    target_in,
    device_in,
    flip_in,
    count_in,
    e,
    h,
    a,
    g,
    sens,
    e_hist,
    a_hist,
    ed,
    ec,
    md,
    mc,
    row_send,
    row_recv,
    col_send,
    col_recv,
    seam_send,
    seam_recv,
    land_send,
    land_recv,
    table,
    entry_row,
    entry_ref,
    entry_sem,
    scatter_mat,
    source_ref,
    target_ref,
    device_ref,
    flip_ref,
    count_ref,
    in_sems,
    map_sems,
    last_row_send,
    last_row_recv,
    last_col_send,
    last_col_recv,
    last_ssem,
    last_rsem,
    row_ssem,
    row_rsem,
    col_ssem,
    col_rsem,
    seam_ssem,
    seam_rsem,
    land_sems,
):
    layers, cc, ca = shape
    halves = ca // LANES
    subs = cc // 8
    n_dev = n_circ * n_axial
    rows = n_dev * CAP * 2
    cols = 2 * halves * cc
    blocks = halves * cc
    ci = lax.axis_index("circ")
    ai = lax.axis_index("axial")
    me = ci * n_axial + ai

    barrier = pltpu.get_barrier_semaphore()
    partners = [(dc, da) for dc in reversed(range(n_circ)) for da in reversed(range(n_axial)) if dc or da]
    far = [(dc, da) for dc, da in partners if da]
    near = [(dc, da) for dc, da in partners if not da]

    def peer_of(dc, da):
        flip = jnp.where((ai == 1) | (ai == 2), 1, 0) if da >= 2 else 0
        return lax.bitwise_xor(ci, dc), lax.bitwise_xor(lax.bitwise_xor(ai, da), flip)

    col_recv[...] = jnp.zeros_like(col_recv)
    last_col_recv[...] = jnp.zeros_like(last_col_recv)
    for dc, da in partners:
        pl.semaphore_signal(barrier, inc=1, device_id=peer_of(dc, da), device_id_type=MESH)

    loads = [
        pltpu.make_async_copy(src, dst, in_sems.at[i])
        for i, (src, dst) in enumerate(
            [
                (e_in, e),
                (g_in, g),
                (a_in, a),
                (ed_in, ed),
                (ec_in, ec),
                (md_in, md),
                (mc_in, mc),
                (h_in, h),
                (e_in, e_hist.at[0]),
            ]
        )
    ]
    maps = [
        pltpu.make_async_copy(src, dst, map_sems.at[i])
        for i, (src, dst) in enumerate(
            [
                (source_in, source_ref),
                (target_in, target_ref),
                (device_in, device_ref),
                (flip_in, flip_ref),
                (count_in, count_ref),
            ]
        )
    ]
    for load in maps + loads:
        load.start()

    def send_all(send, recv, ssem, rsem, group):
        for dc, da in group:
            pc, pa = peer_of(dc, da)
            pltpu.make_async_remote_copy(
                src_ref=send.at[pc * n_axial + pa],
                dst_ref=recv.at[me],
                send_sem=ssem,
                recv_sem=rsem,
                device_id=(pc, pa),
                device_id_type=MESH,
            ).start()

    def keep_own(send, recv):
        recv[pl.ds(me, 1)] = send[pl.ds(me, 1)]

    def all_to_all_done(send, recv, ssem, rsem):
        return pltpu.make_async_remote_copy(
            src_ref=send.at[pl.ds(0, n_dev - 1)],
            dst_ref=recv.at[pl.ds(0, n_dev - 1)],
            send_sem=ssem,
            recv_sem=rsem,
            device_id=(ci, ai),
            device_id_type=MESH,
        )

    lane8 = lax.broadcasted_iota(jnp.int32, (8, LANES), 1)

    def row_copy(kind, t, step):
        peer = lax.rem(ci + step + n_circ, n_circ)
        return pltpu.make_async_remote_copy(
            src_ref=row_send.at[kind, t],
            dst_ref=row_recv.at[kind, t],
            send_sem=row_ssem.at[kind, t],
            recv_sem=row_rsem.at[kind, t],
            device_id=(peer, ai),
            device_id_type=MESH,
        )

    def col_copy(kind, t, step):
        peer = lax.rem(ai + step + n_axial, n_axial)
        return pltpu.make_async_remote_copy(
            src_ref=col_send.at[kind, t],
            dst_ref=col_recv.at[kind, t],
            send_sem=col_ssem.at[kind, t],
            recv_sem=col_rsem.at[kind, t],
            device_id=(ci, peer),
            device_id_type=MESH,
        )

    def pack_halos(field, kind, t, step, levels):
        edge_row = 0 if step < 0 else cc - 1
        for part, c in enumerate((0, 2)):
            for l in levels:
                at = part * layers + l
                row_send[kind, t, at : at + 1, :] = field[c, l, edge_row : edge_row + 1, :]
        col_send[kind, t] = pack_column(
            field, step, [((c * layers + l) * subs, c, l) for c in range(2) for l in levels]
        )

    def pack_column(field, step, places):
        packed = jnp.zeros((8, LANES), jnp.float32)
        for first, c, l in places:
            for s in range(subs):
                k = first + s
                lo = 0 if step < 0 else ca - LANES
                tile = field[c, l, s * 8 : s * 8 + 8, lo : lo + LANES]
                shift = k if step < 0 else (k + 1) % LANES
                if shift:
                    tile = pltpu.roll(tile, shift, 1)
                packed = jnp.where(lane8 == k, tile, packed)
        return packed

    def last_copies(q, t, step):
        row = pltpu.make_async_remote_copy(
            src_ref=last_row_send.at[q, t],
            dst_ref=last_row_recv.at[q, t],
            send_sem=last_ssem.at[q, t, 0],
            recv_sem=last_rsem.at[q, t, 0],
            device_id=(lax.rem(ci + step + n_circ, n_circ), ai),
            device_id_type=MESH,
        )
        col = pltpu.make_async_remote_copy(
            src_ref=last_col_send.at[q, t],
            dst_ref=last_col_recv.at[q, t],
            send_sem=last_ssem.at[q, t, 1],
            recv_sem=last_rsem.at[q, t, 1],
            device_id=(ci, lax.rem(ai + step + n_axial, n_axial)),
            device_id_type=MESH,
        )
        return row, col

    def pack_last(field, q, t):
        for part, c in enumerate((0, 2)):
            last_row_send[q, t, part : part + 1, :] = field[c, layers - 1, cc - 1 : cc, :]
        last_col_send[q, t] = pack_column(field, 1, [(c * subs, c, layers - 1) for c in range(2)])

    def start_last(q, t):
        row, col = last_copies(q, t, 1)
        row.start()
        pl.when(ai < n_axial - 1)(col.start)

    def wait_last(q, t):
        row, col = last_copies(q, t, 1)
        row.wait_recv()
        pl.when(ai > 0)(col.wait_recv)

    def drain_last(q, t):
        row, col = last_copies(q, t, 1)
        row.wait_send()
        pl.when(ai < n_axial - 1)(col.wait_send)

    def start_halos(kind, t, step):
        row_copy(kind, t, step).start()

        @pl.when((ai > 0) if step < 0 else (ai < n_axial - 1))
        def _():
            col_copy(kind, t, step).start()

    def wait_halos(kind, t, step):
        row_copy(kind, t, step).wait_recv()

        @pl.when((ai < n_axial - 1) if step < 0 else (ai > 0))
        def _():
            col_copy(kind, t, step).wait_recv()

    def drain_halos(kind, t, step):
        row_copy(kind, t, step).wait_send()

        @pl.when((ai > 0) if step < 0 else (ai < n_axial - 1))
        def _():
            col_copy(kind, t, step).wait_send()

    def fill_table(field):
        ends = LANES - 1 - lax.broadcasted_iota(jnp.int32, (cc, LANES), 1)
        for c in (1, 2):
            for h in range(halves):
                face = field[c, layers - 1, :, h * LANES : (h + 1) * LANES]
                turned = jnp.take_along_axis(face, ends, axis=1)
                at = 2 * h + c - 1
                table[pl.ds(at, cc, stride=2 * halves), :] = face
                table[pl.ds(2 * blocks + at, cc, stride=2 * halves), :] = -turned if c == 2 else turned

    def rows_of(peer, slot):
        entry = jnp.clip(entry_ref[0, peer * CAP + slot], 0, 2 * blocks)
        return table[pl.ds(2 * entry, 2), :]

    def send_seams(chain, t, group):
        send, recv = seam_send.at[chain, t], seam_recv.at[chain, t]
        for dc, da in group:
            pc, pa = peer_of(dc, da)
            peer = pc * n_axial + pa
            for slot in range(CAP):
                send[peer, 2 * slot : 2 * slot + 2] = rows_of(peer, slot)
            pltpu.make_async_remote_copy(
                src_ref=send.at[peer],
                dst_ref=recv.at[me],
                send_sem=seam_ssem.at[chain, t],
                recv_sem=seam_rsem.at[chain, t],
                device_id=(pc, pa),
                device_id_type=MESH,
            ).start()
        if group is not far:
            for slot in range(CAP):
                recv[me, 2 * slot : 2 * slot + 2] = rows_of(me, slot)

    def ghosts_of(chain, t):
        send, recv = seam_send.at[chain, t], seam_recv.at[chain, t]
        all_to_all_done(send, recv, seam_ssem.at[chain, t], seam_rsem.at[chain, t]).wait_recv()
        ghosts = picked_dot(scatter_mat[...], recv[...].reshape(rows, LANES))
        return [
            jnp.concatenate(
                [
                    ghosts[(c * halves + h) * cc : (c * halves + h + 1) * cc]
                    for h in range(halves)
                ],
                axis=1,
            )
            for c in range(2)
        ]

    sub = lax.broadcasted_iota(jnp.int32, (cc, ca), 0)
    lane = lax.broadcasted_iota(jnp.int32, (cc, ca), 1)

    def column_halo(packed, first, last):
        parts = []
        for s in range(subs):
            k = first + s
            shift = (LANES - 1 - k if last else -k) % LANES
            parts.append(pltpu.roll(packed, shift, 1) if shift else packed)
        halo = jnp.concatenate(parts, axis=0)
        return jnp.concatenate([halo] * halves, axis=1)

    def metric(diagonal, coupling, l, x, y, z):
        d0, d1, d2 = (diagonal[i, l] for i in range(3))
        o0, o1, o2 = (coupling[i, l] for i in range(3))
        return (
            d0 * x + o0 * y + o1 * z,
            o0 * x + d1 * y + o2 * z,
            o1 * x + o2 * y + d2 * z,
        )

    def forward_update(field, new, kind, t, scale, levels):
        packed = col_recv[kind, t]
        for l in levels:
            v0, v1, v2 = (field[i, l] for i in range(3))
            inside = l + 1 < layers
            r1 = (field[1, l + 1] if inside else 0.0) - v1
            r2 = (field[2, l + 1] if inside else 0.0) - v2

            def around(v, part):
                row = row_recv[kind, t, part * layers + l : part * layers + l + 1, :]
                return jnp.where(sub == cc - 1, row, pltpu.roll(v, cc - 1, 0)) - v

            def along(v, c):
                halo = column_halo(packed, (c * layers + l) * subs, True)
                return jnp.where(lane == ca - 1, halo, pltpu.roll(v, ca - 1, 1)) - v

            x = around(v2, 1) - along(v1, 1)
            y = along(v0, 0) - r2
            z = r1 - around(v0, 0)
            change = metric(md, mc, l, x, y, z)
            for i in range(3):
                new[i, l] = new[i, l] + scale * change[i]

    def add_rim(new, chain, t, scale):
        g0, g1 = ghosts_of(chain, t)
        change = metric(md, mc, layers - 1, 0.0, -g1, g0)
        for i in range(3):
            new[i, layers - 1] = new[i, layers - 1] + scale * change[i]

    def backward_update(field, new, kept, kind, t, scale, levels):
        packed = col_recv[kind, t]
        for l in levels:
            v0, v1, v2 = (field[i, l] for i in range(3))

            def around(v, part):
                if l == layers - 1:
                    return v - jnp.where(sub == 0, 0.0, pltpu.roll(v, 1, 0))
                row = row_recv[kind, t, part * layers + l : part * layers + l + 1, :]
                return v - jnp.where(sub == 0, row, pltpu.roll(v, 1, 0))

            def along(v, c):
                if l == layers - 1:
                    return v - jnp.where(lane == 0, 0.0, pltpu.roll(v, 1, 1))
                halo = column_halo(packed, (c * layers + l) * subs, False)
                return v - jnp.where(lane == 0, halo, pltpu.roll(v, 1, 1))

            r1 = v1 - field[1, l - 1] if l else v1
            r2 = v2 - field[2, l - 1] if l else v2
            x = around(v2, 1) - along(v1, 1)
            y = along(v0, 0) - r2
            z = r1 - around(v0, 0)
            change = metric(ed, ec, l, x, y, z)
            for i in range(3):
                value = new[i, l] + scale * change[i]
                new[i, l] = value
                if kept is not None:
                    kept[i, l] = value

    def add_halo(new, kept, q, t, scale):
        packed = last_col_recv[q, t]
        row0, row2 = (
            jnp.where(sub == 0, last_row_recv[q, t, part : part + 1, :], 0.0) for part in range(2)
        )
        col0, col1 = (
            jnp.where(lane == 0, column_halo(packed, c * subs, False), 0.0) for c in range(2)
        )
        change = metric(ed, ec, layers - 1, col1 - row2, -col0, row0)
        for i in range(3):
            value = new[i, layers - 1] + scale * change[i]
            new[i, layers - 1] = value
            if kept is not None:
                kept[i, layers - 1] = value

    seams = source_ref.shape[1]
    for load in maps:
        load.wait()
    device = device_ref[...]
    count = count_ref[0]
    slot_row = lax.broadcasted_iota(jnp.int32, (1, seams), 1)
    si = lax.broadcasted_iota(jnp.int32, (seams, seams), 0)
    sj = lax.broadcasted_iota(jnp.int32, (seams, seams), 1)
    device_f = device.astype(jnp.float32)
    device_col = jnp.sum(
        jnp.where(si == sj, jnp.broadcast_to(device_f, (seams, seams)), 0.0), axis=1, keepdims=True
    )
    earlier = (device_col == device_f) & (si < sj)
    rank = jnp.sum(jnp.where(earlier, 1.0, 0.0), axis=0, keepdims=True)
    code = jnp.where(slot_row < count, device_f * CAP + rank, -1.0)
    ri = lax.broadcasted_iota(jnp.int32, (rows, seams), 0)
    place = lax.div(ri, 2).astype(jnp.float32) == code

    def picked(values):
        return jnp.sum(
            jnp.where(place, values.astype(jnp.float32), 0.0), axis=1, keepdims=True
        ).astype(jnp.int32)

    comp = lax.rem(lax.broadcasted_iota(jnp.int32, (rows, 1), 0), 2)

    def column_of(block):
        return (comp * halves + lax.rem(block, halves)) * cc + lax.div(block, halves)

    valid = jnp.sum(jnp.where(place, 1.0, 0.0), axis=1, keepdims=True) > 0.5
    landing = jnp.where(valid, column_of(picked(target_ref[...])), -1).astype(jnp.float32)
    group_lane = lax.broadcasted_iota(jnp.int32, (rows, LANES), 1)
    own_lane = group_lane == lax.rem(lax.broadcasted_iota(jnp.int32, (rows, LANES), 0), 2 * CAP)
    spots = jnp.where(own_lane, landing, 0.0).reshape(n_dev, 2 * CAP, LANES)
    land_send[...] = jnp.sum(spots, axis=1, keepdims=True)

    def upright(row):
        spread = jnp.broadcast_to(row.astype(jnp.float32), (seams, seams))
        return jnp.sum(jnp.where(si == sj, spread, 0.0), axis=1, keepdims=True)

    width = entry_row.shape[1]
    slot_lane = lax.broadcasted_iota(jnp.int32, (seams, width), 1).astype(jnp.float32)
    aimed = slot_lane == upright(code)
    taken = upright(source_ref[...] + blocks * flip_ref[...])
    entry = jnp.sum(jnp.where(aimed, taken, 0.0), axis=0, keepdims=True)
    live = jnp.sum(jnp.where(aimed, 1.0, 0.0), axis=0, keepdims=True) > 0.5
    entry_row[...] = jnp.where(live, entry, 2.0 * blocks).astype(jnp.int32)
    entries = pltpu.make_async_copy(entry_row, entry_ref, entry_sem.at[0])
    entries.start()
    table[pl.ds(4 * blocks, 8), :] = jnp.zeros((8, LANES), jnp.float32)

    inner, last = list(range(layers - 1)), [layers - 1]
    loads[0].wait()
    fill_table(e)
    entries.wait()
    pack_halos(e, EF, 0, -1, inner + last)
    loads[1].wait()
    pack_halos(g, GB, 0, 1, inner)
    pack_last(g, 1, 0)
    pl.semaphore_wait(barrier, n_dev - 1)
    start_last(1, 0)
    start_halos(GB, 0, 1)
    start_halos(EF, 0, -1)
    for partner in partners:
        send_all(land_send, land_recv, land_sems.at[0], land_sems.at[1], [partner])
    send_seams(0, 0, partners)
    keep_own(land_send, land_recv)
    for load in loads[2:]:
        load.wait()
    backward_update(g, a, None, GB, 0, -TIME_STEP, last)

    def step(t, carry):
        wait_last(1, t)
        add_halo(a, a_hist.at[STEPS - 1 - t], 1, t, -TIME_STEP)
        fill_table(a)
        send_seams(1, t, far)
        wait_halos(GB, t, 1)
        backward_update(g, a, a_hist.at[STEPS - 1 - t], GB, t, -TIME_STEP, inner)
        pack_halos(a, AF, t, -1, inner + last)
        start_halos(AF, t, -1)
        send_seams(1, t, near)

        @pl.when(t == 0)
        def _():
            all_to_all_done(land_send, land_recv, land_sems.at[0], land_sems.at[1]).wait_recv()
            came = jnp.broadcast_to(land_recv[...], (n_dev, 2 * CAP, LANES)).reshape(rows, LANES)
            spot = jnp.sum(jnp.where(own_lane, came, 0.0), axis=1, keepdims=True)
            spread = jnp.where(spot == group_lane.astype(jnp.float32), 1.0, 0.0)
            scatter = spread.T[:cols].astype(jnp.bfloat16)
            scatter_mat[...] = jnp.concatenate([scatter] * 3, axis=1)

        wait_halos(EF, t, -1)
        forward_update(e, h, EF, t, -TIME_STEP, inner + last)
        pack_halos(h, HB, t, 1, inner)
        start_halos(HB, t, 1)
        add_rim(h, 0, t, -TIME_STEP)
        pack_last(h, 0, t)
        start_last(0, t)
        backward_update(h, e, None, HB, t, TIME_STEP, last)

        @pl.when(t == STEPS - 1)
        def _():
            for l in range(layers):
                for i in range(3):
                    total = e_hist[STEPS - 1, i, l] * a_hist[STEPS - 1, i, l]
                    for n in reversed(range(STEPS - 1)):
                        total = total + e_hist[n, i, l] * a_hist[n, i, l]
                    sens[i, l] = total

        wait_halos(AF, t, -1)
        forward_update(a, g, AF, t, TIME_STEP, inner + last)

        @pl.when(t + 1 < STEPS)
        def _():
            pack_halos(g, GB, t + 1, 1, inner)
            start_halos(GB, t + 1, 1)

        add_rim(g, 1, t, TIME_STEP)

        @pl.when(t + 1 < STEPS)
        def _():
            pack_last(g, 1, t + 1)
            start_last(1, t + 1)
            backward_update(g, a, None, GB, t, -TIME_STEP, last)
            wait_last(0, t)
            add_halo(e, e_hist.at[t + 1], 0, t, TIME_STEP)
            fill_table(e)
            send_seams(0, t + 1, far)
            wait_halos(HB, t, 1)
            backward_update(h, e, e_hist.at[t + 1], HB, t, TIME_STEP, inner)
            pack_halos(e, EF, t + 1, -1, inner + last)
            start_halos(EF, t + 1, -1)
            send_seams(0, t + 1, near)

        return carry

    lax.fori_loop(0, STEPS, step, 0)

    def drain(t, carry):
        for kind, way in ((EF, -1), (HB, 1), (AF, -1), (GB, 1)):
            drain_halos(kind, t, way)
        drain_last(1, t)
        for chain in range(2):
            all_to_all_done(
                seam_send.at[chain, t],
                seam_recv.at[chain, t],
                seam_ssem.at[chain, t],
                seam_rsem.at[chain, t],
            ).wait_send()
        return carry

    lax.fori_loop(0, STEPS, drain, 0)
    all_to_all_done(land_send, land_recv, land_sems.at[0], land_sems.at[1]).wait_send()
    wait_halos(HB, STEPS - 1, 1)
    backward_update(h, e, None, HB, STEPS - 1, TIME_STEP, inner)
    wait_last(0, STEPS - 1)
    add_halo(e, None, 0, STEPS - 1, TIME_STEP)
    for t in range(STEPS):
        drain_last(0, t)


def copy_out(*refs):
    sources, targets, sems = refs[:5], refs[5:10], refs[10]
    stores = [
        pltpu.make_async_copy(src, dst, sems.at[i])
        for i, (src, dst) in enumerate(zip(sources, targets))
    ]
    for store in stores:
        store.start()
    for store in stores:
        store.wait()


def shards(n_circ, n_axial, *args):
    fields, (source, target, device, flip, count) = args[:8], args[8:]
    block = fields[0].shape
    layers, cc, ca = block[1:]
    n_dev = n_circ * n_axial
    rows = n_dev * CAP * 2
    cols = 2 * (ca // LANES) * cc
    width = -(-n_dev * CAP // LANES) * LANES
    operands = [*fields, source, target, device.reshape(1, -1), flip]
    f32 = jnp.float32
    dma = pltpu.SemaphoreType.DMA
    hbm_spec = pl.BlockSpec(memory_space=pltpu.HBM)
    vmem_spec = pl.BlockSpec(memory_space=pltpu.VMEM)
    results = pl.pallas_call(
        functools.partial(kernel, (layers, cc, ca), n_circ, n_axial),
        out_shape=[pltpu.VMEM(block, f32)] * 5,
        in_specs=[hbm_spec] * 12 + [pl.BlockSpec(memory_space=pl.ANY)],
        out_specs=[vmem_spec] * 5,
        scratch_shapes= [pltpu.VMEM((STEPS,) + block, f32)] * 2
        + [pltpu.VMEM(block, f32)] * 4
        + [pltpu.VMEM((4, STEPS, 2 * layers, ca), f32)] * 2
        + [pltpu.VMEM((4, STEPS, 8, LANES), f32)] * 2
        + [pltpu.VMEM((2, STEPS, n_dev, 2 * CAP, LANES), f32)] * 2
        + [pltpu.VMEM((n_dev, 1, LANES), f32)] * 2
        + [pltpu.VMEM((4 * (ca // LANES) * cc + 8, LANES), f32)]
        + [pltpu.VMEM((1, width), jnp.int32), pltpu.SMEM((1, width), jnp.int32), dma((1,))]
        + [pltpu.VMEM((cols, 3 * rows), jnp.bfloat16)]
        + [pltpu.VMEM(source.shape, jnp.int32)] * 4
        + [pltpu.SMEM(count.shape, jnp.int32)]
        + [dma((9,)), dma((5,))]
        + [pltpu.VMEM((2, STEPS, 2, ca), f32)] * 2
        + [pltpu.VMEM((2, STEPS, 8, LANES), f32)] * 2
        + [dma((2, STEPS, 2))] * 2
        + [dma((4, STEPS))] * 4
        + [dma((2, STEPS))] * 2
        + [dma((2,))],
        compiler_params=pltpu.CompilerParams(
            collective_id=0, has_side_effects=True, vmem_limit_bytes=48 << 20
        ),
    )(*[pltpu.with_memory_space_constraint(x, pltpu.HBM) for x in operands], count)
    return pl.pallas_call(
        copy_out,
        out_shape=[jax.ShapeDtypeStruct(block, f32)] * 5,
        in_specs=[vmem_spec] * 5,
        out_specs=[hbm_spec] * 5,
        scratch_shapes=[dma((5,))],
    )(*[pltpu.with_memory_space_constraint(x, pltpu.VMEM) for x in results])


def solution(mesh):
    field = P(None, None, "circ", "axial")
    both = ("circ", "axial")
    return jax.shard_map(
        functools.partial(shards, mesh.shape["circ"], mesh.shape["axial"]),
        mesh=mesh,
        in_specs=(field,) * 8
        + (P(both, None), P(both, None), P(both, None, None), P(both, None), P(both)),
        out_specs=(field,) * 5,
        check_vma=False,
    )
```

```python
import functools

import jax
import jax.numpy as jnp
from jax import lax
from jax.experimental import pallas as pl
from jax.experimental.pallas import tpu as pltpu
from jax.sharding import PartitionSpec as P

STEPS = 4
CAP = 2
TIME_STEP = 0.18
MESH = pl.DeviceIdType.MESH
LANES = 128

EF, HB, AF, GB = range(4)


def pieces(x):
    high = x.astype(jnp.bfloat16)
    rest = x - high.astype(jnp.float32)
    mid = rest.astype(jnp.bfloat16)
    low = (rest - mid.astype(jnp.float32)).astype(jnp.bfloat16)
    return jnp.concatenate([high, mid, low], axis=0)


def picked_dot(matrix, x):
    return jnp.dot(matrix, pieces(x), preferred_element_type=jnp.float32)


def kernel(
    shape,
    n_circ,
    n_axial,
    e_in,
    h_in,
    a_in,
    g_in,
    ed_in,
    ec_in,
    md_in,
    mc_in,
    source_in,
    target_in,
    device_in,
    flip_in,
    count_in,
    e,
    h,
    a,
    g,
    sens,
    e_hist,
    a_hist,
    ed,
    ec,
    md,
    mc,
    row_send,
    row_recv,
    col_send,
    col_recv,
    seam_send,
    seam_recv,
    land_send,
    land_recv,
    table,
    entry_row,
    entry_ref,
    entry_sem,
    scatter_mat,
    source_ref,
    target_ref,
    device_ref,
    flip_ref,
    count_ref,
    in_sems,
    map_sems,
    last_row_send,
    last_row_recv,
    last_col_send,
    last_col_recv,
    last_ssem,
    last_rsem,
    row_ssem,
    row_rsem,
    col_ssem,
    col_rsem,
    seam_ssem,
    seam_rsem,
    land_sems,
):
    layers, cc, ca = shape
    halves = ca // LANES
    subs = cc // 8
    n_dev = n_circ * n_axial
    rows = n_dev * CAP * 2
    cols = 2 * halves * cc
    blocks = halves * cc
    ci = lax.axis_index("circ")
    ai = lax.axis_index("axial")
    me = ci * n_axial + ai

    barrier = pltpu.get_barrier_semaphore()
    partners = [(dc, da) for dc in reversed(range(n_circ)) for da in reversed(range(n_axial)) if dc or da]
    far = [(dc, da) for dc, da in partners if da]
    near = [(dc, da) for dc, da in partners if not da]

    def peer_of(dc, da):
        flip = jnp.where((ai == 1) | (ai == 2), 1, 0) if da >= 2 else 0
        return lax.bitwise_xor(ci, dc), lax.bitwise_xor(lax.bitwise_xor(ai, da), flip)

    col_recv[...] = jnp.zeros_like(col_recv)
    last_col_recv[...] = jnp.zeros_like(last_col_recv)
    for dc, da in partners:
        pl.semaphore_signal(barrier, inc=1, device_id=peer_of(dc, da), device_id_type=MESH)

    loads = [
        pltpu.make_async_copy(src, dst, in_sems.at[i])
        for i, (src, dst) in enumerate(
            [
                (e_in, e),
                (g_in, g),
                (a_in, a),
                (ed_in, ed),
                (ec_in, ec),
                (md_in, md),
                (mc_in, mc),
                (h_in, h),
                (e_in, e_hist.at[0]),
            ]
        )
    ]
    maps = [
        pltpu.make_async_copy(src, dst, map_sems.at[i])
        for i, (src, dst) in enumerate(
            [
                (source_in, source_ref),
                (target_in, target_ref),
                (device_in, device_ref),
                (flip_in, flip_ref),
                (count_in, count_ref),
            ]
        )
    ]
    for load in maps + loads:
        load.start()

    def send_all(send, recv, ssem, rsem, group):
        for dc, da in group:
            pc, pa = peer_of(dc, da)
            pltpu.make_async_remote_copy(
                src_ref=send.at[pc * n_axial + pa],
                dst_ref=recv.at[me],
                send_sem=ssem,
                recv_sem=rsem,
                device_id=(pc, pa),
                device_id_type=MESH,
            ).start()

    def keep_own(send, recv):
        recv[pl.ds(me, 1)] = send[pl.ds(me, 1)]

    def all_to_all_done(send, recv, ssem, rsem):
        return pltpu.make_async_remote_copy(
            src_ref=send.at[pl.ds(0, n_dev - 1)],
            dst_ref=recv.at[pl.ds(0, n_dev - 1)],
            send_sem=ssem,
            recv_sem=rsem,
            device_id=(ci, ai),
            device_id_type=MESH,
        )

    lane8 = lax.broadcasted_iota(jnp.int32, (8, LANES), 1)

    def row_copy(kind, t, step):
        peer = lax.rem(ci + step + n_circ, n_circ)
        return pltpu.make_async_remote_copy(
            src_ref=row_send.at[kind, t],
            dst_ref=row_recv.at[kind, t],
            send_sem=row_ssem.at[kind, t],
            recv_sem=row_rsem.at[kind, t],
            device_id=(peer, ai),
            device_id_type=MESH,
        )

    def col_copy(kind, t, step):
        peer = lax.rem(ai + step + n_axial, n_axial)
        return pltpu.make_async_remote_copy(
            src_ref=col_send.at[kind, t],
            dst_ref=col_recv.at[kind, t],
            send_sem=col_ssem.at[kind, t],
            recv_sem=col_rsem.at[kind, t],
            device_id=(ci, peer),
            device_id_type=MESH,
        )

    def pack_halos(field, kind, t, step, levels):
        edge_row = 0 if step < 0 else cc - 1
        for part, c in enumerate((0, 2)):
            for l in levels:
                at = part * layers + l
                row_send[kind, t, at : at + 1, :] = field[c, l, edge_row : edge_row + 1, :]
        col_send[kind, t] = pack_column(
            field, step, [((c * layers + l) * subs, c, l) for c in range(2) for l in levels]
        )

    def pack_column(field, step, places):
        packed = jnp.zeros((8, LANES), jnp.float32)
        for first, c, l in places:
            for s in range(subs):
                k = first + s
                lo = 0 if step < 0 else ca - LANES
                tile = field[c, l, s * 8 : s * 8 + 8, lo : lo + LANES]
                shift = k if step < 0 else (k + 1) % LANES
                if shift:
                    tile = pltpu.roll(tile, shift, 1)
                packed = jnp.where(lane8 == k, tile, packed)
        return packed

    def last_copies(q, t, step):
        row = pltpu.make_async_remote_copy(
            src_ref=last_row_send.at[q, t],
            dst_ref=last_row_recv.at[q, t],
            send_sem=last_ssem.at[q, t, 0],
            recv_sem=last_rsem.at[q, t, 0],
            device_id=(lax.rem(ci + step + n_circ, n_circ), ai),
            device_id_type=MESH,
        )
        col = pltpu.make_async_remote_copy(
            src_ref=last_col_send.at[q, t],
            dst_ref=last_col_recv.at[q, t],
            send_sem=last_ssem.at[q, t, 1],
            recv_sem=last_rsem.at[q, t, 1],
            device_id=(ci, lax.rem(ai + step + n_axial, n_axial)),
            device_id_type=MESH,
        )
        return row, col

    def pack_last(field, q, t):
        for part, c in enumerate((0, 2)):
            last_row_send[q, t, part : part + 1, :] = field[c, layers - 1, cc - 1 : cc, :]
        last_col_send[q, t] = pack_column(field, 1, [(c * subs, c, layers - 1) for c in range(2)])

    def start_last(q, t):
        row, col = last_copies(q, t, 1)
        row.start()
        pl.when(ai < n_axial - 1)(col.start)

    def wait_last(q, t):
        row, col = last_copies(q, t, 1)
        row.wait_recv()
        pl.when(ai > 0)(col.wait_recv)

    def drain_last(q, t):
        row, col = last_copies(q, t, 1)
        row.wait_send()
        pl.when(ai < n_axial - 1)(col.wait_send)

    def start_halos(kind, t, step):
        row_copy(kind, t, step).start()

        @pl.when((ai > 0) if step < 0 else (ai < n_axial - 1))
        def _():
            col_copy(kind, t, step).start()

    def wait_halos(kind, t, step):
        row_copy(kind, t, step).wait_recv()

        @pl.when((ai < n_axial - 1) if step < 0 else (ai > 0))
        def _():
            col_copy(kind, t, step).wait_recv()

    def drain_halos(kind, t, step):
        row_copy(kind, t, step).wait_send()

        @pl.when((ai > 0) if step < 0 else (ai < n_axial - 1))
        def _():
            col_copy(kind, t, step).wait_send()

    def fill_table(field):
        ends = LANES - 1 - lax.broadcasted_iota(jnp.int32, (cc, LANES), 1)
        for c in (1, 2):
            for h in range(halves):
                face = field[c, layers - 1, :, h * LANES : (h + 1) * LANES]
                turned = jnp.take_along_axis(face, ends, axis=1)
                at = 2 * h + c - 1
                table[pl.ds(at, cc, stride=2 * halves), :] = face
                table[pl.ds(2 * blocks + at, cc, stride=2 * halves), :] = -turned if c == 2 else turned

    def rows_of(peer, slot):
        entry = jnp.clip(entry_ref[0, peer * CAP + slot], 0, 2 * blocks)
        return table[pl.ds(2 * entry, 2), :]

    def send_seams(chain, t, group):
        send, recv = seam_send.at[chain, t], seam_recv.at[chain, t]
        for dc, da in group:
            pc, pa = peer_of(dc, da)
            peer = pc * n_axial + pa
            for slot in range(CAP):
                send[peer, 2 * slot : 2 * slot + 2] = rows_of(peer, slot)
            pltpu.make_async_remote_copy(
                src_ref=send.at[peer],
                dst_ref=recv.at[me],
                send_sem=seam_ssem.at[chain, t],
                recv_sem=seam_rsem.at[chain, t],
                device_id=(pc, pa),
                device_id_type=MESH,
            ).start()
        if group is not far:
            for slot in range(CAP):
                recv[me, 2 * slot : 2 * slot + 2] = rows_of(me, slot)

    def ghosts_of(chain, t):
        send, recv = seam_send.at[chain, t], seam_recv.at[chain, t]
        all_to_all_done(send, recv, seam_ssem.at[chain, t], seam_rsem.at[chain, t]).wait_recv()
        ghosts = picked_dot(scatter_mat[...], recv[...].reshape(rows, LANES))
        return [
            jnp.concatenate(
                [
                    ghosts[(c * halves + h) * cc : (c * halves + h + 1) * cc]
                    for h in range(halves)
                ],
                axis=1,
            )
            for c in range(2)
        ]

    sub = lax.broadcasted_iota(jnp.int32, (cc, ca), 0)
    lane = lax.broadcasted_iota(jnp.int32, (cc, ca), 1)

    def column_halo(packed, first, last):
        parts = []
        for s in range(subs):
            k = first + s
            shift = (LANES - 1 - k if last else -k) % LANES
            parts.append(pltpu.roll(packed, shift, 1) if shift else packed)
        halo = jnp.concatenate(parts, axis=0)
        return jnp.concatenate([halo] * halves, axis=1)

    def metric(diagonal, coupling, l, x, y, z):
        d0, d1, d2 = (diagonal[i, l] for i in range(3))
        o0, o1, o2 = (coupling[i, l] for i in range(3))
        return (
            d0 * x + o0 * y + o1 * z,
            o0 * x + d1 * y + o2 * z,
            o1 * x + o2 * y + d2 * z,
        )

    def forward_update(field, new, kind, t, scale, levels):
        packed = col_recv[kind, t]
        for l in levels:
            v0, v1, v2 = (field[i, l] for i in range(3))
            inside = l + 1 < layers
            r1 = (field[1, l + 1] if inside else 0.0) - v1
            r2 = (field[2, l + 1] if inside else 0.0) - v2

            def around(v, part):
                row = row_recv[kind, t, part * layers + l : part * layers + l + 1, :]
                return jnp.where(sub == cc - 1, row, pltpu.roll(v, cc - 1, 0)) - v

            def along(v, c):
                halo = column_halo(packed, (c * layers + l) * subs, True)
                return jnp.where(lane == ca - 1, halo, pltpu.roll(v, ca - 1, 1)) - v

            x = around(v2, 1) - along(v1, 1)
            y = along(v0, 0) - r2
            z = r1 - around(v0, 0)
            change = metric(md, mc, l, x, y, z)
            for i in range(3):
                new[i, l] = new[i, l] + scale * change[i]

    def add_rim(new, chain, t, scale):
        g0, g1 = ghosts_of(chain, t)
        change = metric(md, mc, layers - 1, 0.0, -g1, g0)
        for i in range(3):
            new[i, layers - 1] = new[i, layers - 1] + scale * change[i]

    def backward_update(field, new, kept, kind, t, scale, levels):
        packed = col_recv[kind, t]
        for l in levels:
            v0, v1, v2 = (field[i, l] for i in range(3))

            def around(v, part):
                if l == layers - 1:
                    return v - jnp.where(sub == 0, 0.0, pltpu.roll(v, 1, 0))
                row = row_recv[kind, t, part * layers + l : part * layers + l + 1, :]
                return v - jnp.where(sub == 0, row, pltpu.roll(v, 1, 0))

            def along(v, c):
                if l == layers - 1:
                    return v - jnp.where(lane == 0, 0.0, pltpu.roll(v, 1, 1))
                halo = column_halo(packed, (c * layers + l) * subs, False)
                return v - jnp.where(lane == 0, halo, pltpu.roll(v, 1, 1))

            r1 = v1 - field[1, l - 1] if l else v1
            r2 = v2 - field[2, l - 1] if l else v2
            x = around(v2, 1) - along(v1, 1)
            y = along(v0, 0) - r2
            z = r1 - around(v0, 0)
            change = metric(ed, ec, l, x, y, z)
            for i in range(3):
                value = new[i, l] + scale * change[i]
                new[i, l] = value
                if kept is not None:
                    kept[i, l] = value

    def add_halo(new, kept, q, t, scale):
        packed = last_col_recv[q, t]
        row0, row2 = (
            jnp.where(sub == 0, last_row_recv[q, t, part : part + 1, :], 0.0) for part in range(2)
        )
        col0, col1 = (
            jnp.where(lane == 0, column_halo(packed, c * subs, False), 0.0) for c in range(2)
        )
        change = metric(ed, ec, layers - 1, col1 - row2, -col0, row0)
        for i in range(3):
            value = new[i, layers - 1] + scale * change[i]
            new[i, layers - 1] = value
            if kept is not None:
                kept[i, layers - 1] = value

    seams = source_ref.shape[1]
    for load in maps:
        load.wait()
    device = device_ref[...]
    count = count_ref[0]
    slot_row = lax.broadcasted_iota(jnp.int32, (1, seams), 1)
    si = lax.broadcasted_iota(jnp.int32, (seams, seams), 0)
    sj = lax.broadcasted_iota(jnp.int32, (seams, seams), 1)
    device_f = device.astype(jnp.float32)
    device_col = jnp.sum(
        jnp.where(si == sj, jnp.broadcast_to(device_f, (seams, seams)), 0.0), axis=1, keepdims=True
    )
    earlier = (device_col == device_f) & (si < sj)
    rank = jnp.sum(jnp.where(earlier, 1.0, 0.0), axis=0, keepdims=True)
    code = jnp.where(slot_row < count, device_f * CAP + rank, -1.0)
    ri = lax.broadcasted_iota(jnp.int32, (rows, seams), 0)
    place = lax.div(ri, 2).astype(jnp.float32) == code

    def picked(values):
        return jnp.sum(
            jnp.where(place, values.astype(jnp.float32), 0.0), axis=1, keepdims=True
        ).astype(jnp.int32)

    comp = lax.rem(lax.broadcasted_iota(jnp.int32, (rows, 1), 0), 2)

    def column_of(block):
        return (comp * halves + lax.rem(block, halves)) * cc + lax.div(block, halves)

    valid = jnp.sum(jnp.where(place, 1.0, 0.0), axis=1, keepdims=True) > 0.5
    landing = jnp.where(valid, column_of(picked(target_ref[...])), -1).astype(jnp.float32)
    group_lane = lax.broadcasted_iota(jnp.int32, (rows, LANES), 1)
    own_lane = group_lane == lax.rem(lax.broadcasted_iota(jnp.int32, (rows, LANES), 0), 2 * CAP)
    spots = jnp.where(own_lane, landing, 0.0).reshape(n_dev, 2 * CAP, LANES)
    land_send[...] = jnp.sum(spots, axis=1, keepdims=True)

    def upright(row):
        spread = jnp.broadcast_to(row.astype(jnp.float32), (seams, seams))
        return jnp.sum(jnp.where(si == sj, spread, 0.0), axis=1, keepdims=True)

    width = entry_row.shape[1]
    slot_lane = lax.broadcasted_iota(jnp.int32, (seams, width), 1).astype(jnp.float32)
    aimed = slot_lane == upright(code)
    taken = upright(source_ref[...] + blocks * flip_ref[...])
    entry = jnp.sum(jnp.where(aimed, taken, 0.0), axis=0, keepdims=True)
    live = jnp.sum(jnp.where(aimed, 1.0, 0.0), axis=0, keepdims=True) > 0.5
    entry_row[...] = jnp.where(live, entry, 2.0 * blocks).astype(jnp.int32)
    entries = pltpu.make_async_copy(entry_row, entry_ref, entry_sem.at[0])
    entries.start()
    table[pl.ds(4 * blocks, 8), :] = jnp.zeros((8, LANES), jnp.float32)

    inner, last = list(range(layers - 1)), [layers - 1]
    loads[0].wait()
    fill_table(e)
    entries.wait()
    pack_halos(e, EF, 0, -1, inner + last)
    loads[1].wait()
    pack_halos(g, GB, 0, 1, inner)
    pack_last(g, 1, 0)
    pl.semaphore_wait(barrier, n_dev - 1)
    start_last(1, 0)
    start_halos(GB, 0, 1)
    start_halos(EF, 0, -1)
    for partner in partners:
        send_all(land_send, land_recv, land_sems.at[0], land_sems.at[1], [partner])
    send_seams(0, 0, partners)
    keep_own(land_send, land_recv)
    for load in loads[2:]:
        load.wait()
    backward_update(g, a, None, GB, 0, -TIME_STEP, last)

    def step(t, carry):
        wait_last(1, t)
        add_halo(a, a_hist.at[STEPS - 1 - t], 1, t, -TIME_STEP)
        fill_table(a)
        send_seams(1, t, far)
        wait_halos(GB, t, 1)
        backward_update(g, a, a_hist.at[STEPS - 1 - t], GB, t, -TIME_STEP, inner)
        pack_halos(a, AF, t, -1, inner + last)
        start_halos(AF, t, -1)
        send_seams(1, t, near)

        @pl.when(t == 0)
        def _():
            all_to_all_done(land_send, land_recv, land_sems.at[0], land_sems.at[1]).wait_recv()
            came = jnp.broadcast_to(land_recv[...], (n_dev, 2 * CAP, LANES)).reshape(rows, LANES)
            spot = jnp.sum(jnp.where(own_lane, came, 0.0), axis=1, keepdims=True)
            spread = jnp.where(spot == group_lane.astype(jnp.float32), 1.0, 0.0)
            scatter = spread.T[:cols].astype(jnp.bfloat16)
            scatter_mat[...] = jnp.concatenate([scatter] * 3, axis=1)

        wait_halos(EF, t, -1)
        forward_update(e, h, EF, t, -TIME_STEP, inner + last)
        pack_halos(h, HB, t, 1, inner)
        start_halos(HB, t, 1)
        add_rim(h, 0, t, -TIME_STEP)
        pack_last(h, 0, t)
        start_last(0, t)
        backward_update(h, e, None, HB, t, TIME_STEP, last)

        @pl.when(t == STEPS - 1)
        def _():
            for l in range(layers):
                for i in range(3):
                    total = e_hist[STEPS - 1, i, l] * a_hist[STEPS - 1, i, l]
                    for n in reversed(range(STEPS - 1)):
                        total = total + e_hist[n, i, l] * a_hist[n, i, l]
                    sens[i, l] = total

        wait_halos(AF, t, -1)
        forward_update(a, g, AF, t, TIME_STEP, inner + last)

        @pl.when(t + 1 < STEPS)
        def _():
            pack_halos(g, GB, t + 1, 1, inner)
            start_halos(GB, t + 1, 1)

        add_rim(g, 1, t, TIME_STEP)

        @pl.when(t + 1 < STEPS)
        def _():
            pack_last(g, 1, t + 1)
            start_last(1, t + 1)
            backward_update(g, a, None, GB, t, -TIME_STEP, last)
            wait_last(0, t)
            add_halo(e, e_hist.at[t + 1], 0, t, TIME_STEP)
            fill_table(e)
            send_seams(0, t + 1, far)
            wait_halos(HB, t, 1)
            backward_update(h, e, e_hist.at[t + 1], HB, t, TIME_STEP, inner)
            pack_halos(e, EF, t + 1, -1, inner + last)
            start_halos(EF, t + 1, -1)
            send_seams(0, t + 1, near)

        return carry

    lax.fori_loop(0, STEPS, step, 0)

    def drain(t, carry):
        for kind, way in ((EF, -1), (HB, 1), (AF, -1), (GB, 1)):
            drain_halos(kind, t, way)
        drain_last(1, t)
        pl.when(t < STEPS - 1)(lambda: drain_last(0, t))
        for chain in range(2):
            all_to_all_done(
                seam_send.at[chain, t],
                seam_recv.at[chain, t],
                seam_ssem.at[chain, t],
                seam_rsem.at[chain, t],
            ).wait_send()
        return carry

    lax.fori_loop(0, STEPS, drain, 0)
    all_to_all_done(land_send, land_recv, land_sems.at[0], land_sems.at[1]).wait_send()
    wait_halos(HB, STEPS - 1, 1)
    backward_update(h, e, None, HB, STEPS - 1, TIME_STEP, inner)
    wait_last(0, STEPS - 1)
    add_halo(e, None, 0, STEPS - 1, TIME_STEP)
    drain_last(0, STEPS - 1)


def copy_out(*refs):
    sources, targets, sems = refs[:5], refs[5:10], refs[10]
    stores = [
        pltpu.make_async_copy(src, dst, sems.at[i])
        for i, (src, dst) in enumerate(zip(sources, targets))
    ]
    for store in stores:
        store.start()
    for store in stores:
        store.wait()


def shards(n_circ, n_axial, *args):
    fields, (source, target, device, flip, count) = args[:8], args[8:]
    block = fields[0].shape
    layers, cc, ca = block[1:]
    n_dev = n_circ * n_axial
    rows = n_dev * CAP * 2
    cols = 2 * (ca // LANES) * cc
    width = -(-n_dev * CAP // LANES) * LANES
    operands = [*fields, source, target, device.reshape(1, -1), flip]
    f32 = jnp.float32
    dma = pltpu.SemaphoreType.DMA
    hbm_spec = pl.BlockSpec(memory_space=pltpu.HBM)
    vmem_spec = pl.BlockSpec(memory_space=pltpu.VMEM)
    results = pl.pallas_call(
        functools.partial(kernel, (layers, cc, ca), n_circ, n_axial),
        out_shape=[pltpu.VMEM(block, f32)] * 5,
        in_specs=[hbm_spec] * 12 + [pl.BlockSpec(memory_space=pl.ANY)],
        out_specs=[vmem_spec] * 5,
        scratch_shapes= [pltpu.VMEM((STEPS,) + block, f32)] * 2
        + [pltpu.VMEM(block, f32)] * 4
        + [pltpu.VMEM((4, STEPS, 2 * layers, ca), f32)] * 2
        + [pltpu.VMEM((4, STEPS, 8, LANES), f32)] * 2
        + [pltpu.VMEM((2, STEPS, n_dev, 2 * CAP, LANES), f32)] * 2
        + [pltpu.VMEM((n_dev, 1, LANES), f32)] * 2
        + [pltpu.VMEM((4 * (ca // LANES) * cc + 8, LANES), f32)]
        + [pltpu.VMEM((1, width), jnp.int32), pltpu.SMEM((1, width), jnp.int32), dma((1,))]
        + [pltpu.VMEM((cols, 3 * rows), jnp.bfloat16)]
        + [pltpu.VMEM(source.shape, jnp.int32)] * 4
        + [pltpu.SMEM(count.shape, jnp.int32)]
        + [dma((9,)), dma((5,))]
        + [pltpu.VMEM((2, STEPS, 2, ca), f32)] * 2
        + [pltpu.VMEM((2, STEPS, 8, LANES), f32)] * 2
        + [dma((2, STEPS, 2))] * 2
        + [dma((4, STEPS))] * 4
        + [dma((2, STEPS))] * 2
        + [dma((2,))],
        compiler_params=pltpu.CompilerParams(
            collective_id=0, has_side_effects=True, vmem_limit_bytes=48 << 20
        ),
    )(*[pltpu.with_memory_space_constraint(x, pltpu.HBM) for x in operands], count)
    return pl.pallas_call(
        copy_out,
        out_shape=[jax.ShapeDtypeStruct(block, f32)] * 5,
        in_specs=[vmem_spec] * 5,
        out_specs=[hbm_spec] * 5,
        scratch_shapes=[dma((5,))],
    )(*[pltpu.with_memory_space_constraint(x, pltpu.VMEM) for x in results])


def solution(mesh):
    field = P(None, None, "circ", "axial")
    both = ("circ", "axial")
    return jax.shard_map(
        functools.partial(shards, mesh.shape["circ"], mesh.shape["axial"]),
        mesh=mesh,
        in_specs=(field,) * 8
        + (P(both, None), P(both, None), P(both, None, None), P(both, None), P(both)),
        out_specs=(field,) * 5,
        check_vma=False,
    )
```
